32 devices in a mesh: expert: 4 (over x, core), group: 8 (over z, y).
Axes of the slice: x: 2, y: 2, z: 4, core: 2. Of those that a mesh axis runs over, the one named last changes fastest.
Arguments:
- tokens: bfloat16 [16384, 2048], P(('expert', 'group')), may hold values from -6 to 6
- routing: int32 [16384, 8], P(('expert', 'group')), may hold values from 0 to 31, as said below
- mixing: float32 [16384, 8], P(('expert', 'group')), may hold values from 0.1 to 1
- visited: int32 [4], replicated, may hold values from 0 to 31, as said below
- gate_matrix: bfloat16 [32, 2048, 768], P('expert', 'group'), may hold values from -0.125 to 0.125
- up_matrix: bfloat16 [32, 2048, 768], P('expert', 'group'), may hold values from -0.125 to 0.125
- down_matrix: bfloat16 [32, 768, 2048], P('expert', None, 'group'), may hold values from -0.21875 to 0.21875
Outputs:
- combined: bfloat16 [16384, 2048], P(('expert', 'group'))
The draws below stay inside these ranges and needn't reach their ends.
Inputs may be any that keep to these rules, and one draw needn't show every extreme that they name: `routing`: each row names 8 different experts. In the rows of one device, each expert of visited is named by at least half of 80 (rounded up) and at most 80 rows, and for each visited expert some device has exactly 80 such rows. `visited`: 4 different experts.
All inputs are finite; a program needn't handle non-finite values.
Results may differ from the reference program's by a relative error of at most 0.0049.
Values may be sent and summed in bfloat16 or wider, within the bound.
No kernel may reach another device: no remote copies, remote signals or barrier semaphores. Data moves between devices by JAX's collectives and lax.ppermute only.
A program may use at most 128 MiB of HBM per device.

```python
import jax
import jax.numpy as jnp
from jax import lax

D = 2048
FF = 768
TOP = 8
VISITS = 4
ROWS_DEV = 512
CAP = 80
EXPERTS = 32
ROWS = 16384


def routing_tables(key):
    middle = jax.random.permutation(jax.random.fold_in(key, 11), EXPERTS - 2) + 1
    ends = jnp.array([0, EXPERTS - 1], dtype=middle.dtype)
    order = jnp.concatenate([ends, middle])
    mixed_front = jax.random.permutation(jax.random.fold_in(key, 17), VISITS)
    chosen = order[:VISITS][mixed_front]
    others = order[VISITS:]
    blocks = ROWS // ROWS_DEV
    loads = jax.random.randint(jax.random.fold_in(key, 12), (blocks, VISITS), (CAP + 1) // 2, CAP + 1)
    fullest = jax.random.randint(jax.random.fold_in(key, 13), (VISITS,), 0, blocks)
    loads = jnp.where(jnp.arange(blocks)[:, None] == fullest[None, :], CAP, loads)
    scores = jax.random.randint(jax.random.fold_in(key, 14), (blocks, VISITS, ROWS_DEV), 0, 1 << 20)
    scores = scores * ROWS_DEV + jnp.arange(ROWS_DEV)[None, None, :]
    ranks = jnp.argsort(jnp.argsort(scores, axis=2), axis=2)
    member = (ranks < loads[:, :, None]).transpose(0, 2, 1).reshape(ROWS, VISITS)
    spare = EXPERTS - VISITS
    offsets = jax.random.randint(jax.random.fold_in(key, 15), (ROWS,), 0, spare)
    table = others[(offsets[:, None] + jnp.arange(TOP)[None, :]) % spare]
    for number in range(VISITS):
        table = table.at[:, number].set(jnp.where(member[:, number], chosen[number], table[:, number]))
    shuffle_keys = jax.random.randint(jax.random.fold_in(key, 16), (ROWS, TOP), 0, 1 << 20)
    shuffle_keys = shuffle_keys * TOP + jnp.arange(TOP)[None, :]
    shuffle = jnp.argsort(shuffle_keys, axis=1)
    return (chosen.astype(jnp.int32), jnp.take_along_axis(table, shuffle, axis=1).astype(jnp.int32))


def draw_routing(key, part):
    return routing_tables(key)[1]


def draw_visited(key, part):
    return routing_tables(key)[0]


def block_scale(own_key, shape, cuts, smallest, high):
    gain, own = 1.0, jax.random.fold_in(own_key, 6)
    for position, blocks in cuts:
        draws = jnp.exp(jax.random.uniform(jax.random.fold_in(own, position), (blocks,), jnp.float32, smallest / len(cuts), high / len(cuts)))
        gain = gain * jnp.repeat(draws, shape[position] // blocks).reshape([-1 if axis == position else 1 for axis in range(len(shape))])
    return gain


def scatter_about(stream_key, shape, spread, bound, pieces=(), kind=jnp.bfloat16):
    factor_of = block_scale(stream_key, shape, pieces, -0.22, 0.18) if pieces else 1.0
    entries = jax.random.normal(stream_key, shape, jnp.float32) * spread * factor_of
    return jnp.minimum(jnp.maximum(entries, -bound), bound).astype(kind)


def setup_inputs(seed: int = 0) -> dict:
    key_list = jax.random.split(jax.random.key(seed), 8)
    return {
        "tokens": scatter_about(key_list[0], (ROWS, D), 1.0, 6.0, ((0, 32),)),
        "routing": draw_routing(jax.random.fold_in(key_list[7], 71), 0),
        "mixing": jnp.clip(0.1 + 0.9 * jax.random.uniform(key_list[2], (ROWS, TOP), jnp.float32) ** block_scale(key_list[2], (ROWS, TOP), ((0, 32),), -0.2, 0.2), 0.1, 1.0),
        "visited": draw_visited(jax.random.fold_in(key_list[7], 71), 0),
        "gate_matrix": scatter_about(key_list[4], (EXPERTS, D, FF), D ** -0.5, 0.125, ((0, 4), (1, 8))),
        "up_matrix": scatter_about(key_list[5], (EXPERTS, D, FF), D ** -0.5, 0.125, ((0, 4), (1, 8))),
        "down_matrix": scatter_about(key_list[6], (EXPERTS, FF, D), FF ** -0.5, 0.21875, ((0, 4), (2, 8))),
    }


def select_rows(routing, mixing, target, capacity):
    hit = routing == target
    member = jnp.any(hit, axis=1)
    share = jnp.sum(jnp.where(hit, mixing, jnp.zeros_like(mixing)), axis=1)
    place = jnp.cumsum(member.astype(jnp.int32)) - 1
    slots = jnp.arange(capacity, dtype=jnp.int32)
    table = member[:, None] & (place[:, None] == slots[None, :])
    indices = jnp.arange(routing.shape[0], dtype=jnp.int32)
    rows = jnp.sum(jnp.where(table, indices[:, None], 0), axis=0).astype(jnp.int32)
    filled = jnp.any(table, axis=0)
    scales = jnp.where(filled, share[rows], jnp.zeros_like(share[rows]))
    return rows, scales


def reference(tokens, routing, mixing, visited, gate_matrix, up_matrix, down_matrix):
    blocks = tokens.shape[0] // ROWS_DEV
    token_blocks = tokens.reshape(blocks, ROWS_DEV, D)
    route_blocks = routing.reshape(blocks, ROWS_DEV, TOP)
    mix_blocks = mixing.reshape(blocks, ROWS_DEV, TOP)
    experts = []
    for number in range(VISITS):
        target = visited[number]
        experts.append((gate_matrix[target].astype(jnp.float32), up_matrix[target].astype(jnp.float32),
                        down_matrix[target].astype(jnp.float32)))

    def one_block(packed):
        block_tokens, block_routing, block_mixing = packed
        total = jnp.zeros((ROWS_DEV, D), jnp.float32)
        for number in range(VISITS):
            gate_full, up_full, down_full = experts[number]
            rows, scales = select_rows(block_routing, block_mixing, visited[number], CAP)
            picked = block_tokens[rows].astype(jnp.float32)
            gate = jnp.dot(picked, gate_full, precision=lax.Precision.HIGHEST)
            up = jnp.dot(picked, up_full, precision=lax.Precision.HIGHEST)
            hidden = lax.optimization_barrier((jax.nn.silu(gate) * up).astype(jnp.bfloat16))
            output = jnp.dot(hidden.astype(jnp.float32), down_full, precision=lax.Precision.HIGHEST)
            total = total.at[rows].add(scales[:, None] * output)
        return total

    result = lax.map(one_block, (token_blocks, route_blocks, mix_blocks))
    return result.reshape(tokens.shape[0], D).astype(jnp.bfloat16)
```

```python
import functools

import jax
import jax.numpy as jnp
from jax import lax
from jax.experimental import pallas as pl
from jax.experimental.pallas import tpu as pltpu
from jax.sharding import PartitionSpec as P

VISITS = 4
CAP = 80
AXES = ("expert", "group")
F32 = jnp.float32
BF16 = jnp.bfloat16


VMEM = pl.BlockSpec(memory_space=pltpu.VMEM)
SMEM = pl.BlockSpec(memory_space=pltpu.SMEM)
ANY = pl.BlockSpec(memory_space=pl.ANY)


def pick_kernel(order, routing, mixing, tokens, *outs):
    picks, high, low = outs[:VISITS], outs[VISITS], outs[VISITS + 1]
    rows = tokens.shape[0]
    lanes = lax.broadcasted_iota(jnp.int32, (rows, 128), 1)
    named, mix = routing[...], mixing[...]
    shares, members = [], jnp.zeros((rows, 128), F32)
    for k in range(VISITS):
        hit = named == order[k]
        shares.append(jnp.sum(jnp.where(hit, mix, 0.0), axis=1, keepdims=True))
        found = jnp.sum(jnp.where(hit, 1.0, 0.0), axis=1, keepdims=True)
        members = members + jnp.where(lanes == k, found, 0.0)
    above = lax.broadcasted_iota(jnp.int32, (rows, rows), 0) > lax.broadcasted_iota(
        jnp.int32, (rows, rows), 1
    )
    ranks = jnp.dot(
        jnp.where(above, 1.0, 0.0).astype(BF16), members.astype(BF16), preferred_element_type=F32
    )
    places = jnp.where(members > 0.5, ranks + (lanes * CAP).astype(F32), -1.0)
    slots = lax.broadcasted_iota(jnp.int32, (rows, VISITS * CAP), 1).astype(F32)
    spread = jnp.zeros((rows, VISITS * CAP), F32)
    for k in range(VISITS):
        spread = spread + jnp.where(slots == places[:, k : k + 1], shares[k], 0.0)
    top = spread.astype(BF16)
    high[...] = top
    low[...] = (spread - top.astype(F32)).astype(BF16)
    across = places.T
    slots = lax.broadcasted_iota(jnp.int32, (CAP, rows), 0).astype(F32)
    for k in range(VISITS):
        one = jnp.where(slots + float(CAP * k) == across[k : k + 1, :], 1.0, 0.0).astype(BF16)
        picks[k][...] = jnp.dot(one, tokens[...], preferred_element_type=F32).astype(BF16)


def pick(order, routing, mixing, tokens):
    rows, width = tokens.shape
    return pl.pallas_call(
        pick_kernel,
        out_shape=[jax.ShapeDtypeStruct((CAP, width), BF16)] * VISITS
        + [jax.ShapeDtypeStruct((rows, VISITS * CAP), BF16)] * 2,
        in_specs=[SMEM, VMEM, VMEM, VMEM],
        out_specs=[VMEM] * (VISITS + 2),
        compiler_params=pltpu.CompilerParams(vmem_limit_bytes=40 << 20),
        name="pick",
    )(order, routing, mixing, tokens)


def merge_kernel(high, low, *refs):
    pieces, out = refs[:VISITS], refs[VISITS]
    values = jnp.concatenate([piece[...] for piece in pieces], axis=0)
    total = jnp.dot(high[...], values, preferred_element_type=F32)
    total = total + jnp.dot(low[...], values, preferred_element_type=F32)
    out[...] = total.astype(BF16)


def merge(high, low, pieces):
    rows, width = high.shape[0], pieces[0].shape[1]
    tile = 512
    whole = pl.BlockSpec(high.shape, lambda i: (0, 0))
    return pl.pallas_call(
        merge_kernel,
        grid=(width // tile,),
        out_shape=jax.ShapeDtypeStruct((rows, width), BF16),
        in_specs=[whole, whole] + [pl.BlockSpec((CAP, tile), lambda i: (0, i))] * VISITS,
        out_specs=pl.BlockSpec((rows, tile), lambda i: (0, i)),
        compiler_params=pltpu.CompilerParams(vmem_limit_bytes=40 << 20),
        name="merge",
    )(high, low, *pieces)


def load_blocks(blocks, starts, held, sem, down):
    copies = []
    for n, block in enumerate(blocks):
        first = pl.multiple_of(starts[2 * n], 64)
        rows = pl.ds(first, block.shape[1])
        if down:
            second = pl.multiple_of(starts[2 * n + 1], 128)
            place = held.at[rows, pl.ds(second, block.shape[2])]
        else:
            place = held.at[rows, :]
        copies.append(pltpu.make_async_copy(block.at[0], place, sem.at[n]))
    for copy in copies:
        copy.start()
    for copy in copies:
        copy.wait()


def gate_kernel(count, starts, *refs):
    blocks, rows, out, held, sem = refs[:count], refs[count : count + VISITS], *refs[count + VISITS :]
    load_blocks(blocks, starts, held, sem, False)
    picked = jnp.concatenate([ref[...] for ref in rows], axis=0)
    out[...] = jnp.dot(picked, held[...], preferred_element_type=F32)


def up_kernel(count, starts, *refs):
    blocks, rows = refs[:count], refs[count : count + VISITS]
    gate, out, held, sem = refs[count + VISITS :]
    load_blocks(blocks, starts, held, sem, False)
    picked = jnp.concatenate([ref[...] for ref in rows], axis=0)
    up = jnp.dot(picked, held[...], preferred_element_type=F32)
    out[...] = (jax.nn.silu(gate[...]) * up).astype(BF16)


def down_kernel(count, starts, *refs):
    blocks, hidden, outs = refs[:count], refs[count], refs[count + 1 : count + 1 + VISITS]
    held, sem = refs[count + 1 + VISITS :]
    load_blocks(blocks, starts, held, sem, True)
    for k in range(VISITS):
        part = hidden[pl.ds(k * CAP, CAP), :]
        outs[k][...] = jnp.dot(part, held[...], preferred_element_type=F32).astype(BF16)


def compute(kernel, starts, blocks, others, out_shape, matrix, name):
    count = len(blocks)
    many = isinstance(out_shape, list)
    return pl.pallas_call(
        functools.partial(kernel, count),
        out_shape=out_shape,
        in_specs=[SMEM] + [ANY] * count + [VMEM] * len(others),
        out_specs=[VMEM] * len(out_shape) if many else VMEM,
        scratch_shapes=[pltpu.VMEM(matrix, BF16), pltpu.SemaphoreType.DMA((count,))],
        compiler_params=pltpu.CompilerParams(vmem_limit_bytes=40 << 20),
        name=name,
    )(starts, *blocks, *others)


def body(mesh, tokens, routing, mixing, visited, gate_matrix, up_matrix, down_matrix):
    experts, groups = mesh.shape["expert"], mesh.shape["group"]
    planes = VISITS
    sides = groups // planes
    held = gate_matrix.shape[0]
    width, inner = tokens.shape[1], gate_matrix.shape[2]
    e, g = lax.axis_index("expert"), lax.axis_index("group")
    c, x = e & 1, (e >> 1) & 1
    z, y = g // sides, g % sides
    ab = (z ^ (z >> 1)) & 1

    def swap(value, expert_bits=0, plane_bits=0, side_bits=0):
        pairs = []
        for one in range(experts):
            for two in range(groups):
                other = ((two // sides) ^ plane_bits) * sides + ((two % sides) ^ side_bits)
                pairs.append((one * groups + two, (one ^ expert_bits) * groups + other))
        return lax.ppermute(value, AXES, pairs)

    numbers = [2 * ab + x, 2 * (1 - ab) + x, 2 * ab + 1 - x, 2 * (1 - ab) + 1 - x]
    order = visited[jnp.stack(numbers)]
    owners, locals_ = order // held, order % held

    *picked, high, low = pick(order, routing, mixing, tokens)
    rows = [
        picked[0],
        swap(picked[1], plane_bits=1),
        swap(picked[2], expert_bits=2),
        swap(picked[3], expert_bits=2, plane_bits=1),
    ]

    def gather_blocks(matrix):
        half, columns = matrix.shape[1] // 2, matrix.shape[2]

        def block(k, h):
            return lax.dynamic_slice(matrix, (locals_[k], h * half, 0), (1, half, columns))

        mine = [block(k, c) for k in range(VISITS)]
        theirs = [block(k, 1 - c) for k in range(VISITS)]
        bit = 4
        while bit < experts:
            both = jnp.concatenate(mine + theirs, axis=0)
            got = swap(both, expert_bits=bit)
            ours = [(owners[k] & bit) == (e & bit) for k in range(VISITS)]
            mine = [jnp.where(ours[k], mine[k], got[k][None]) for k in range(VISITS)]
            theirs = [jnp.where(ours[k], theirs[k], got[VISITS + k][None]) for k in range(VISITS)]
            bit *= 2
        got = swap(jnp.concatenate(theirs, axis=0), expert_bits=1)
        mine = [jnp.where((owners[k] & 1) == c, mine[k], got[k][None]) for k in range(VISITS)]
        got = swap(jnp.concatenate(mine[2:], axis=0), expert_bits=2)
        same, other = (
            jnp.where(((owners[k] >> 1) & 1) == x, mine[k], got[k][None]) for k in range(2)
        )
        found = [
            (0, same),
            (1, swap(other, plane_bits=1)),
            (2, swap(other, plane_bits=2)),
            (3, swap(same, plane_bits=3)),
        ]
        blocks = []
        for plane_bits, value in found:
            for side_bits in range(sides):
                moved = value if side_bits == 0 else swap(value, side_bits=side_bits)
                blocks.append((plane_bits, side_bits, 0, moved))
                blocks.append((plane_bits, side_bits, 1, swap(moved, expert_bits=1)))
        starts = []
        for plane_bits, side_bits, core, _ in blocks:
            piece = (z ^ plane_bits) * sides + (y ^ side_bits)
            part = (c ^ core) * half
            if matrix.shape[1] == inner:
                starts += [part, piece * columns]
            else:
                starts += [piece * 2 * half + part, jnp.int32(0)]
        return jnp.stack(starts).astype(jnp.int32), [value for *_, value in blocks]

    total = VISITS * CAP
    starts, blocks = gather_blocks(gate_matrix)
    gate = compute(
        gate_kernel, starts, blocks, rows, jax.ShapeDtypeStruct((total, inner), F32), (width, inner), "gate"
    )
    starts, blocks = gather_blocks(up_matrix)
    hidden = compute(
        up_kernel,
        starts,
        blocks,
        rows + [gate],
        jax.ShapeDtypeStruct((total, inner), BF16),
        (width, inner),
        "up",
    )
    starts, blocks = gather_blocks(down_matrix)
    outs = compute(
        down_kernel,
        starts,
        blocks,
        [hidden],
        [jax.ShapeDtypeStruct((CAP, width), BF16)] * VISITS,
        (inner, width),
        "down",
    )
    back = [
        outs[0],
        swap(outs[1], plane_bits=1),
        swap(outs[2], expert_bits=2),
        swap(outs[3], expert_bits=2, plane_bits=1),
    ]
    return merge(high, low, back)


def solution(mesh):
    placed = (
        P(("expert", "group"), None),
        P(("expert", "group"), None),
        P(("expert", "group"), None),
        P(),
        P("expert", "group", None),
        P("expert", "group", None),
        P("expert", None, "group"),
    )
    return jax.shard_map(
        functools.partial(body, mesh),
        mesh=mesh,
        in_specs=placed,
        out_specs=P(("expert", "group"), None),
        check_vma=False,
    )
```

```python
import functools

import jax
import jax.numpy as jnp
from jax import lax
from jax.experimental import pallas as pl
from jax.experimental.pallas import tpu as pltpu
from jax.sharding import PartitionSpec as P

VISITS = 4
CAP = 80
AXES = ("expert", "group")
F32 = jnp.float32
BF16 = jnp.bfloat16


VMEM = pl.BlockSpec(memory_space=pltpu.VMEM)
SMEM = pl.BlockSpec(memory_space=pltpu.SMEM)
ANY = pl.BlockSpec(memory_space=pl.ANY)
HBM = pl.BlockSpec(memory_space=pltpu.HBM)


def place(sides):
    e, g = lax.axis_index("expert"), lax.axis_index("group")
    z = g // sides
    return e, e & 1, (e >> 1) & 1, z, g % sides, (z ^ (z >> 1)) & 1


def visit(k, x, ab):
    return 2 * (ab if k % 2 == 0 else 1 - ab) + (x if k < 2 else 1 - x)


def call(kernel, out_shape, in_specs, args, scratch=(), limit=16, name=None, flops=0, size=0):
    many = isinstance(out_shape, list)
    return pl.pallas_call(
        kernel,
        out_shape=out_shape,
        in_specs=in_specs,
        out_specs=[VMEM] * len(out_shape) if many else VMEM,
        scratch_shapes=list(scratch),
        compiler_params=pltpu.CompilerParams(vmem_limit_bytes=limit << 20),
        cost_estimate=pl.CostEstimate(flops=flops, bytes_accessed=size, transcendentals=0),
        name=name,
    )(*args)


def pick_kernel(sides, visited, routing, mixing, tokens, *outs):
    picks, high, low = outs[:VISITS], outs[VISITS], outs[VISITS + 1]
    _, _, x, _, _, ab = place(sides)
    rows = tokens.shape[0]
    lanes = lax.broadcasted_iota(jnp.int32, (rows, 128), 1)
    named, mix = routing[...], mixing[...]
    shares, members = [], jnp.zeros((rows, 128), F32)
    for k in range(VISITS):
        hit = named == visited[visit(k, x, ab)]
        shares.append(jnp.sum(jnp.where(hit, mix, 0.0), axis=1, keepdims=True))
        found = jnp.sum(jnp.where(hit, 1.0, 0.0), axis=1, keepdims=True)
        members = members + jnp.where(lanes == k, found, 0.0)
    above = lax.broadcasted_iota(jnp.int32, (rows, rows), 0) > lax.broadcasted_iota(
        jnp.int32, (rows, rows), 1
    )
    ranks = jnp.dot(
        jnp.where(above, 1.0, 0.0).astype(BF16), members.astype(BF16), preferred_element_type=F32
    )
    places = jnp.where(members > 0.5, ranks + (lanes * CAP).astype(F32), -1.0)
    slots = lax.broadcasted_iota(jnp.int32, (rows, VISITS * CAP), 1).astype(F32)
    spread = jnp.zeros((rows, VISITS * CAP), F32)
    for k in range(VISITS):
        spread = spread + jnp.where(slots == places[:, k : k + 1], shares[k], 0.0)
    top = spread.astype(BF16)
    high[...] = top
    low[...] = (spread - top.astype(F32)).astype(BF16)
    across = places.T
    slots = lax.broadcasted_iota(jnp.int32, (CAP, rows), 0).astype(F32)
    for k in range(VISITS):
        one = jnp.where(slots + float(CAP * k) == across[k : k + 1, :], 1.0, 0.0).astype(BF16)
        picks[k][...] = jnp.dot(one, tokens[...], preferred_element_type=F32).astype(BF16)


def merge_kernel(high, low, *refs):
    pieces, out = refs[:VISITS], refs[VISITS]
    values = jnp.concatenate([piece[...] for piece in pieces], axis=0)
    total = jnp.dot(high[...], values, preferred_element_type=F32)
    total = total + jnp.dot(low[...], values, preferred_element_type=F32)
    out[...] = total.astype(BF16)


def merge(high, low, pieces):
    rows, width = high.shape[0], pieces[0].shape[1]
    tile = 512
    whole = pl.BlockSpec(high.shape, lambda i: (0, 0))
    return pl.pallas_call(
        merge_kernel,
        grid=(width // tile,),
        out_shape=jax.ShapeDtypeStruct((rows, width), BF16),
        in_specs=[whole, whole] + [pl.BlockSpec((CAP, tile), lambda i: (0, i))] * VISITS,
        out_specs=pl.BlockSpec((rows, tile), lambda i: (0, i)),
        compiler_params=pltpu.CompilerParams(vmem_limit_bytes=16 << 20),
        name="merge",
    )(high, low, *pieces)


def cut_kernel(sides, held, axes, visited, *refs):
    count = len(axes)
    matrices, outs, sem = refs[:count], refs[count : 3 * count], refs[3 * count]
    _, c, x, _, _, ab = place(sides)
    copies = []
    for n, axis in enumerate(axes):
        mine, theirs = outs[2 * n], outs[2 * n + 1]
        size = mine.shape[axis + 1]
        for k in range(VISITS):
            local = lax.rem(visited[visit(k, x, ab)], held)
            for out, half in ((theirs, 1 - c), (mine, c)):
                part = pl.ds(pl.multiple_of(half * size, 128), size)
                source = matrices[n].at[local]
                source = source.at[part, :] if axis == 0 else source.at[:, part]
                copies.append(pltpu.make_async_copy(source, out.at[k], sem.at[len(copies)]))
    for copy in copies:
        copy.start()
    for copy in copies:
        copy.wait()


def cut(sides, visited, matrices, axes, name):
    shapes = []
    for matrix, axis in zip(matrices, axes):
        _, a, b = matrix.shape
        half = (VISITS, a // 2, b) if axis == 0 else (VISITS, a, b // 2)
        shapes += [jax.ShapeDtypeStruct(half, BF16)] * 2
    return call(
        functools.partial(cut_kernel, sides, matrices[0].shape[0], axes),
        shapes,
        [SMEM] + [HBM] * len(matrices),
        (visited, *matrices),
        [pltpu.SemaphoreType.DMA((2 * VISITS * len(matrices),))],
        name=name,
    )


def choose(own, out, here, there):
    @pl.when(own)
    def _():
        out[...] = here[...]

    @pl.when(jnp.logical_not(own))
    def _():
        out[...] = there[...]


def blend_kernel(sides, held, bit, visited, mine, theirs, got, mine_out, theirs_out):
    e, _, x, _, _, ab = place(sides)
    for k in range(VISITS):
        owner = visited[visit(k, x, ab)] // held
        own = (owner & bit) == (e & bit)
        choose(own, mine_out.at[k], mine.at[k], got.at[k])
        choose(own, theirs_out.at[k], theirs.at[k], got.at[VISITS + k])


def send_kernel(sides, held, visited, mine, got, out):
    _, c, x, _, _, ab = place(sides)
    for k in range(2):
        owner = visited[visit(2 + k, x, ab)] // held
        choose((owner & 1) == c, out.at[k], mine.at[2 + k], got.at[2 + k])


def keep_kernel(sides, held, visited, mine, got, far, same, other):
    _, c, x, _, _, ab = place(sides)
    for k, out in enumerate((same, other)):
        owner = visited[visit(k, x, ab)] // held
        near = ((owner >> 1) & 1) == x

        @pl.when(near)
        def _():
            choose((owner & 1) == c, out, mine.at[k], got.at[k])

        @pl.when(jnp.logical_not(near))
        def _():
            out[...] = far[k]


def load_blocks(sides, keys, blocks, held, sem, down):
    _, c, _, z, y, _ = place(sides)
    copies = []
    for n, ((plane_bits, side_bits, core), block) in enumerate(zip(keys, blocks)):
        piece = (z ^ plane_bits) * sides + (y ^ side_bits)
        rows, columns = block.shape
        if down:
            first = pl.ds(pl.multiple_of((c ^ core) * rows, 128), rows)
            spot = held.at[first, pl.ds(pl.multiple_of(piece * columns, 128), columns)]
        else:
            spot = held.at[pl.ds(pl.multiple_of(piece * rows, 128), rows), :]
        copies.append(pltpu.make_async_copy(block, spot, sem.at[n]))
    for copy in copies:
        copy.start()
    for copy in copies:
        copy.wait()


def gate_kernel(sides, keys, *refs):
    blocks, rows = refs[: len(keys)], refs[len(keys) : len(keys) + 2 * VISITS]
    out, held, sem = refs[len(keys) + 2 * VISITS :]
    load_blocks(sides, keys, blocks, held, sem, False)
    for side in range(2):
        picked = jnp.concatenate([ref[...] for ref in rows[side * VISITS : (side + 1) * VISITS]], axis=0)
        out[side] = jnp.dot(picked, held[...], preferred_element_type=F32)


def up_kernel(sides, keys, *refs):
    blocks, rows = refs[: len(keys)], refs[len(keys) : len(keys) + 2 * VISITS]
    gate, own, partner, held, sem = refs[len(keys) + 2 * VISITS :]
    load_blocks(sides, keys, blocks, held, sem, False)
    for side, out in enumerate((own, partner)):
        picked = jnp.concatenate([ref[...] for ref in rows[side * VISITS : (side + 1) * VISITS]], axis=0)
        up = jnp.dot(picked, held[...], preferred_element_type=F32)
        out[...] = (jax.nn.silu(gate[side]) * up).astype(BF16)


def down_kernel(sides, keys, *refs):
    count = len(keys)
    blocks, (own, partner), outs = refs[:count], refs[count : count + 2], refs[count + 2 : count + 2 + VISITS]
    held, hidden, sem = refs[count + 2 + VISITS :]
    _, c, _, _, _, _ = place(sides)
    inner = own.shape[1]
    hidden[:, pl.ds(pl.multiple_of(c * inner, 128), inner)] = own[...]
    hidden[:, pl.ds(pl.multiple_of((1 - c) * inner, 128), inner)] = partner[...]
    load_blocks(sides, keys, blocks, held, sem, True)
    out = jnp.dot(hidden[...], held[...], preferred_element_type=F32).astype(BF16)
    for k in range(VISITS):
        outs[k][...] = out[k * CAP : (k + 1) * CAP]


def body(mesh, tokens, routing, mixing, visited, gate_matrix, up_matrix, down_matrix):
    experts, groups = mesh.shape["expert"], mesh.shape["group"]
    planes = VISITS
    sides = groups // planes
    held = gate_matrix.shape[0]
    count, width = tokens.shape
    inner = gate_matrix.shape[2]
    total = VISITS * CAP
    shape = jax.ShapeDtypeStruct

    def swap(value, expert_bits=0, plane_bits=0, side_bits=0):
        pairs = []
        for one in range(experts):
            for two in range(groups):
                other = ((two // sides) ^ plane_bits) * sides + ((two % sides) ^ side_bits)
                pairs.append((one * groups + two, (one ^ expert_bits) * groups + other))
        return lax.ppermute(value, AXES, pairs)

    halves = list(cut(sides, visited, [gate_matrix], [1], "cut_gate"))
    halves += cut(sides, visited, [up_matrix, down_matrix], [1, 0], "cut_others")
    matrices = []
    for n in range(3):
        mine, theirs = halves[2 * n : 2 * n + 2]
        bit = 4
        while bit < experts:
            got = swap(jnp.concatenate([mine, theirs], axis=0), expert_bits=bit)
            mine, theirs = call(
                functools.partial(blend_kernel, sides, held, bit),
                [shape(mine.shape, BF16)] * 2,
                [SMEM] + [VMEM] * 3,
                (visited, mine, theirs, got),
                limit=32,
                name="blend",
            )
            bit *= 2
        matrices.append((mine, swap(theirs, expert_bits=1)))

    *picked, high, low = call(
        functools.partial(pick_kernel, sides),
        [shape((CAP, width), BF16)] * VISITS + [shape((count, total), BF16)] * 2,
        [SMEM, VMEM, VMEM, VMEM],
        (visited, routing, mixing, tokens),
        limit=24,
        name="pick",
    )

    sent = []
    for mine, got in matrices:
        block = mine.shape[1:]
        away = call(
            functools.partial(send_kernel, sides, held),
            shape((2, *block), BF16),
            [SMEM, VMEM, VMEM],
            (visited, mine, got),
            name="send",
        )
        sent.append(swap(away, expert_bits=2))
    rows = [
        picked[0],
        swap(picked[1], plane_bits=1),
        swap(picked[2], expert_bits=2),
        swap(picked[3], expert_bits=2, plane_bits=1),
    ]

    pieces = []
    for n, (mine, got) in enumerate(matrices):
        block = mine.shape[1:]
        same, other = call(
            functools.partial(keep_kernel, sides, held),
            [shape(block, BF16)] * 2,
            [SMEM] + [VMEM] * 3,
            (visited, mine, got, sent[n]),
            name="keep",
        )
        found = [
            (0, same),
            (1, swap(other, plane_bits=1)),
            (2, swap(other, plane_bits=2)),
            (3, swap(same, plane_bits=3)),
        ]
        keys, blocks = [], []
        for plane_bits, value in found:
            for side_bits in range(sides):
                moved = value if side_bits == 0 else swap(value, side_bits=side_bits)
                keys.append((plane_bits, side_bits, 0))
                blocks.append(moved)
                if n == 2:
                    keys.append((plane_bits, side_bits, 1))
                    blocks.append(swap(moved, expert_bits=1))
        pieces.append((keys, blocks))

    rows += [swap(value, expert_bits=1) for value in rows]
    keys, blocks = pieces[0]
    work = 4 * total * width * inner // 2
    gate = call(
        functools.partial(gate_kernel, sides, keys),
        shape((2, total, inner // 2), F32),
        [ANY] * len(keys) + [VMEM] * len(rows),
        (*blocks, *rows),
        [pltpu.VMEM((width, inner // 2), BF16), pltpu.SemaphoreType.DMA((len(keys),))],
        name="gate",
        flops=work,
    )
    keys, blocks = pieces[1]
    own, partner = call(
        functools.partial(up_kernel, sides, keys),
        [shape((total, inner // 2), BF16)] * 2,
        [ANY] * len(keys) + [VMEM] * (len(rows) + 1),
        (*blocks, *rows, gate),
        [pltpu.VMEM((width, inner // 2), BF16), pltpu.SemaphoreType.DMA((len(keys),))],
        name="up",
        flops=work,
    )
    partner = swap(partner, expert_bits=1)
    keys, blocks = pieces[2]
    outs = call(
        functools.partial(down_kernel, sides, keys),
        [shape((CAP, width), BF16)] * VISITS,
        [ANY] * len(keys) + [VMEM] * 2,
        (*blocks, own, partner),
        [
            pltpu.VMEM((inner, width), BF16),
            pltpu.VMEM((total, inner), BF16),
            pltpu.SemaphoreType.DMA((len(keys),)),
        ],
        name="down",
        flops=work,
    )
    back = [
        outs[0],
        swap(outs[1], plane_bits=1),
        swap(outs[2], expert_bits=2),
        swap(outs[3], expert_bits=2, plane_bits=1),
    ]
    return merge(high, low, back)


def solution(mesh):
    placed = (
        P(("expert", "group"), None),
        P(("expert", "group"), None),
        P(("expert", "group"), None),
        P(),
        P("expert", "group", None),
        P("expert", "group", None),
        P("expert", None, "group"),
    )
    return jax.shard_map(
        functools.partial(body, mesh),
        mesh=mesh,
        in_specs=placed,
        out_specs=P(("expert", "group"), None),
        check_vma=False,
    )
```

```python
import functools

import jax
import jax.numpy as jnp
from jax import lax
from jax.experimental import pallas as pl
from jax.experimental.pallas import tpu as pltpu
from jax.sharding import PartitionSpec as P


VISITS = 4
CAP = 80
AXES = ("expert", "group")
F32 = jnp.float32
BF16 = jnp.bfloat16


VMEM = pl.BlockSpec(memory_space=pltpu.VMEM)
SMEM = pl.BlockSpec(memory_space=pltpu.SMEM)
ANY = pl.BlockSpec(memory_space=pl.ANY)
HBM = pl.BlockSpec(memory_space=pltpu.HBM)


def place(sides):
    e, g = lax.axis_index("expert"), lax.axis_index("group")
    z = g // sides
    return e, e & 1, (e >> 1) & 1, z, g % sides, (z ^ (z >> 1)) & 1


def visit(k, x, ab):
    return 2 * (ab if k % 2 == 0 else 1 - ab) + (x if k < 2 else 1 - x)


def call(kernel, out_shape, in_specs, args, scratch=(), limit=16, flops=0, size=0):
    many = isinstance(out_shape, list)
    return pl.pallas_call(
        kernel,
        out_shape=out_shape,
        in_specs=in_specs,
        out_specs=[VMEM] * len(out_shape) if many else VMEM,
        scratch_shapes=list(scratch),
        compiler_params=pltpu.CompilerParams(vmem_limit_bytes=limit << 20),
        cost_estimate=pl.CostEstimate(flops=flops, bytes_accessed=size, transcendentals=0),
    )(*args)


def pick_kernel(sides, visited, routing, mixing, tokens, *outs):
    picks, high, low = outs[:VISITS], outs[VISITS], outs[VISITS + 1]
    _, _, x, _, _, ab = place(sides)
    rows = tokens.shape[0]
    lanes = lax.broadcasted_iota(jnp.int32, (rows, 128), 1)
    named, mix = routing[...], mixing[...]
    shares, members = [], jnp.zeros((rows, 128), F32)
    for k in range(VISITS):
        hit = named == visited[visit(k, x, ab)]
        shares.append(jnp.sum(jnp.where(hit, mix, 0.0), axis=1, keepdims=True))
        found = jnp.sum(jnp.where(hit, 1.0, 0.0), axis=1, keepdims=True)
        members = members + jnp.where(lanes == k, found, 0.0)
    above = lax.broadcasted_iota(jnp.int32, (rows, rows), 0) > lax.broadcasted_iota(
        jnp.int32, (rows, rows), 1
    )
    ranks = jnp.dot(
        jnp.where(above, 1.0, 0.0).astype(BF16), members.astype(BF16), preferred_element_type=F32
    )
    places = jnp.where(members > 0.5, ranks + (lanes * CAP).astype(F32), -1.0)
    slots = lax.broadcasted_iota(jnp.int32, (rows, VISITS * CAP), 1).astype(F32)
    spread = jnp.zeros((rows, VISITS * CAP), F32)
    for k in range(VISITS):
        spread = spread + jnp.where(slots == places[:, k : k + 1], shares[k], 0.0)
    top = spread.astype(BF16)
    high[...] = top
    low[...] = (spread - top.astype(F32)).astype(BF16)
    across = places.T
    slots = lax.broadcasted_iota(jnp.int32, (CAP, rows), 0).astype(F32)
    for k in range(VISITS):
        one = jnp.where(slots + float(CAP * k) == across[k : k + 1, :], 1.0, 0.0).astype(BF16)
        picks[k][...] = jnp.dot(one, tokens[...], preferred_element_type=F32).astype(BF16)


def merge_kernel(high, low, *refs):
    pieces, out = refs[:VISITS], refs[VISITS]
    values = jnp.concatenate([piece[...] for piece in pieces], axis=0)
    total = jnp.dot(high[...], values, preferred_element_type=F32)
    total = total + jnp.dot(low[...], values, preferred_element_type=F32)
    out[...] = total.astype(BF16)


def merge(high, low, pieces):
    rows, width = high.shape[0], pieces[0].shape[1]
    tile = 512
    whole = pl.BlockSpec(high.shape, lambda i: (0, 0))
    return pl.pallas_call(
        merge_kernel,
        grid=(width // tile,),
        out_shape=jax.ShapeDtypeStruct((rows, width), BF16),
        in_specs=[whole, whole] + [pl.BlockSpec((CAP, tile), lambda i: (0, i))] * VISITS,
        out_specs=pl.BlockSpec((rows, tile), lambda i: (0, i)),
        compiler_params=pltpu.CompilerParams(vmem_limit_bytes=16 << 20),
        name="merge",
    )(high, low, *pieces)


def cut_kernel(sides, held, axes, visited, *refs):
    count = len(axes)
    matrices, outs, sem = refs[:count], refs[count : 3 * count], refs[3 * count]
    _, c, x, _, _, ab = place(sides)
    copies = []
    for n, axis in enumerate(axes):
        mine, theirs = outs[2 * n], outs[2 * n + 1]
        size = mine.shape[axis + 1]
        for k in range(VISITS):
            local = lax.rem(visited[visit(k, x, ab)], held)
            for out, half in ((theirs, 1 - c), (mine, c)):
                part = pl.ds(pl.multiple_of(half * size, 128), size)
                source = matrices[n].at[local]
                source = source.at[part, :] if axis == 0 else source.at[:, part]
                copies.append(pltpu.make_async_copy(source, out.at[k], sem.at[len(copies)]))
    for copy in copies:
        copy.start()
    for copy in copies:
        copy.wait()


def cut(sides, visited, matrices, axes):
    shapes = []
    for matrix, axis in zip(matrices, axes):
        _, a, b = matrix.shape
        half = (VISITS, a // 2, b) if axis == 0 else (VISITS, a, b // 2)
        shapes += [jax.ShapeDtypeStruct(half, BF16)] * 2
    return call(
        functools.partial(cut_kernel, sides, matrices[0].shape[0], axes),
        shapes,
        [SMEM] + [HBM] * len(matrices),
        (visited, *matrices),
        [pltpu.SemaphoreType.DMA((2 * VISITS * len(matrices),))],
    )


def choose(own, out, here, there):
    @pl.when(own)
    def _():
        out[...] = here[...]

    @pl.when(jnp.logical_not(own))
    def _():
        out[...] = there[...]


def blend_kernel(sides, held, bit, visited, mine, theirs, got, mine_out, theirs_out):
    e, _, x, _, _, ab = place(sides)
    for k in range(VISITS):
        owner = visited[visit(k, x, ab)] // held
        own = (owner & bit) == (e & bit)
        choose(own, mine_out.at[k], mine.at[k], got.at[k])
        choose(own, theirs_out.at[k], theirs.at[k], got.at[VISITS + k])


def send_kernel(sides, held, visited, mine, got, out):
    _, c, x, _, _, ab = place(sides)
    for k in range(2):
        owner = visited[visit(2 + k, x, ab)] // held
        choose((owner & 1) == c, out.at[k], mine.at[2 + k], got.at[2 + k])


def keep_kernel(sides, held, visited, mine, got, far, same, other):
    _, c, x, _, _, ab = place(sides)
    for k, out in enumerate((same, other)):
        owner = visited[visit(k, x, ab)] // held
        near = ((owner >> 1) & 1) == x

        @pl.when(near)
        def _():
            choose((owner & 1) == c, out, mine.at[k], got.at[k])

        @pl.when(jnp.logical_not(near))
        def _():
            out[...] = far[k]


def load_blocks(sides, keys, blocks, held, sem, down):
    _, c, _, z, y, _ = place(sides)
    copies = []
    for n, ((plane_bits, side_bits, core), block) in enumerate(zip(keys, blocks)):
        piece = (z ^ plane_bits) * sides + (y ^ side_bits)
        rows, columns = block.shape
        if down:
            first = pl.ds(pl.multiple_of((c ^ core) * rows, 128), rows)
            spot = held.at[first, pl.ds(pl.multiple_of(piece * columns, 128), columns)]
        else:
            spot = held.at[pl.ds(pl.multiple_of(piece * rows, 128), rows), :]
        copies.append(pltpu.make_async_copy(block, spot, sem.at[n]))
    for copy in copies:
        copy.start()
    for copy in copies:
        copy.wait()


def gate_kernel(sides, keys, *refs):
    blocks, rows = refs[: len(keys)], refs[len(keys) : len(keys) + 2 * VISITS]
    out, held, sem = refs[len(keys) + 2 * VISITS :]
    load_blocks(sides, keys, blocks, held, sem, False)
    for side in range(2):
        picked = jnp.concatenate([ref[...] for ref in rows[side * VISITS : (side + 1) * VISITS]], axis=0)
        out[side] = jnp.dot(picked, held[...], preferred_element_type=F32)


def up_kernel(sides, keys, *refs):
    blocks, rows = refs[: len(keys)], refs[len(keys) : len(keys) + 2 * VISITS]
    gate, own, partner, held, sem = refs[len(keys) + 2 * VISITS :]
    load_blocks(sides, keys, blocks, held, sem, False)
    for side, out in enumerate((own, partner)):
        picked = jnp.concatenate([ref[...] for ref in rows[side * VISITS : (side + 1) * VISITS]], axis=0)
        up = jnp.dot(picked, held[...], preferred_element_type=F32)
        out[...] = (jax.nn.silu(gate[side]) * up).astype(BF16)


def down_kernel(sides, keys, *refs):
    count = len(keys)
    blocks, (own, partner), outs = refs[:count], refs[count : count + 2], refs[count + 2 : count + 2 + VISITS]
    held, hidden, sem = refs[count + 2 + VISITS :]
    _, c, _, _, _, _ = place(sides)
    inner = own.shape[1]
    hidden[:, pl.ds(pl.multiple_of(c * inner, 128), inner)] = own[...]
    hidden[:, pl.ds(pl.multiple_of((1 - c) * inner, 128), inner)] = partner[...]
    load_blocks(sides, keys, blocks, held, sem, True)
    out = jnp.dot(hidden[...], held[...], preferred_element_type=F32).astype(BF16)
    for k in range(VISITS):
        outs[k][...] = out[k * CAP : (k + 1) * CAP]


def body(mesh, tokens, routing, mixing, visited, gate_matrix, up_matrix, down_matrix):
    experts, groups = mesh.shape["expert"], mesh.shape["group"]
    planes = VISITS
    sides = groups // planes
    held = gate_matrix.shape[0]
    count, width = tokens.shape
    inner = gate_matrix.shape[2]
    total = VISITS * CAP
    shape = jax.ShapeDtypeStruct

    def swap(value, expert_bits=0, plane_bits=0, side_bits=0):
        pairs = []
        for one in range(experts):
            for two in range(groups):
                other = ((two // sides) ^ plane_bits) * sides + ((two % sides) ^ side_bits)
                pairs.append((one * groups + two, (one ^ expert_bits) * groups + other))
        return lax.ppermute(value, AXES, pairs)

    halves = list(cut(sides, visited, [gate_matrix], [1]))
    halves += cut(sides, visited, [up_matrix, down_matrix], [1, 0])
    matrices = []
    for n in range(3):
        mine, theirs = halves[2 * n : 2 * n + 2]
        bit = 4
        while bit < experts:
            got = swap(jnp.concatenate([mine, theirs], axis=0), expert_bits=bit)
            mine, theirs = call(
                functools.partial(blend_kernel, sides, held, bit),
                [shape(mine.shape, BF16)] * 2,
                [SMEM] + [VMEM] * 3,
                (visited, mine, theirs, got),
                limit=32,
            )
            bit *= 2
        matrices.append((mine, swap(theirs, expert_bits=1)))

    *picked, high, low = call(
        functools.partial(pick_kernel, sides),
        [shape((CAP, width), BF16)] * VISITS + [shape((count, total), BF16)] * 2,
        [SMEM, VMEM, VMEM, VMEM],
        (visited, routing, mixing, tokens),
        limit=24,
    )

    sent = []
    for mine, got in matrices:
        block = mine.shape[1:]
        away = call(
            functools.partial(send_kernel, sides, held),
            shape((2, *block), BF16),
            [SMEM, VMEM, VMEM],
            (visited, mine, got),
        )
        sent.append(swap(away, expert_bits=2))
    rows = [
        picked[0],
        swap(picked[1], plane_bits=1),
        swap(picked[2], expert_bits=2),
        swap(picked[3], expert_bits=2, plane_bits=1),
    ]

    pieces = []
    for n, (mine, got) in enumerate(matrices):
        block = mine.shape[1:]
        same, other = call(
            functools.partial(keep_kernel, sides, held),
            [shape(block, BF16)] * 2,
            [SMEM] + [VMEM] * 3,
            (visited, mine, got, sent[n]),
        )
        found = [
            (0, same), (1, swap(other, plane_bits=1)), (2, swap(other, plane_bits=2)), (3, swap(same, plane_bits=3))
        ]
        keys, blocks = [], []
        for plane_bits, value in found:
            for side_bits in range(sides):
                moved = value
                if side_bits:
                    moved = swap(value, side_bits=side_bits)
                keys.append((plane_bits, side_bits, 0))
                blocks.append(moved)
                if n == 2:
                    keys.append((plane_bits, side_bits, 1))
                    blocks.append(swap(moved, expert_bits=1))
        pieces.append((keys, blocks))

    rows += [swap(value, expert_bits=1) for value in rows]
    keys, blocks = pieces[0]
    work = 4 * total * width * inner // 2
    gate = call(
        functools.partial(gate_kernel, sides, keys),
        shape((2, total, inner // 2), F32),
        [ANY] * len(keys) + [VMEM] * len(rows),
        (*blocks, *rows),
        [pltpu.VMEM((width, inner // 2), BF16), pltpu.SemaphoreType.DMA((len(keys),))],
        flops=work,
    )
    keys, blocks = pieces[1]
    own, partner = call(
        functools.partial(up_kernel, sides, keys),
        [shape((total, inner // 2), BF16)] * 2,
        [ANY] * len(keys) + [VMEM] * (len(rows) + 1),
        (*blocks, *rows, gate),
        [pltpu.VMEM((width, inner // 2), BF16), pltpu.SemaphoreType.DMA((len(keys),))],
        flops=work,
    )
    partner = swap(partner, expert_bits=1)
    keys, blocks = pieces[2]
    outs = call(
        functools.partial(down_kernel, sides, keys),
        [shape((CAP, width), BF16)] * VISITS,
        [ANY] * len(keys) + [VMEM] * 2,
        (*blocks, own, partner),
        [
            pltpu.VMEM((inner, width), BF16),
            pltpu.VMEM((total, inner), BF16),
            pltpu.SemaphoreType.DMA((len(keys),)),
        ],
        flops=work,
    )
    back = [
        outs[0], swap(outs[1], plane_bits=1), swap(outs[2], expert_bits=2), swap(outs[3], expert_bits=2, plane_bits=1)
    ]
    return merge(high, low, back)


def solution(mesh):
    placed = (
        P(("expert", "group"), None),
        P(("expert", "group"), None),
        P(("expert", "group"), None),
        P(),
        P("expert", "group", None),
        P("expert", "group", None),
        P("expert", None, "group"),
    )
    return jax.shard_map(
        functools.partial(body, mesh),
        mesh=mesh,
        in_specs=placed,
        out_specs=P(("expert", "group"), None),
        check_vma=False,
    )
```

```python
import functools

import jax
import jax.numpy as jnp
from jax import lax
from jax.experimental import pallas as pl
from jax.experimental.pallas import tpu as pltpu
from jax.sharding import PartitionSpec as P


VISITS = 4
CAP = 80
AXES = ("expert", "group")
F32 = jnp.float32
BF16 = jnp.bfloat16


STEPS = (((1,), (0,)), ((1, 0),), ((1, 0),))

VMEM = pl.BlockSpec(memory_space=pltpu.VMEM)
SMEM = pl.BlockSpec(memory_space=pltpu.SMEM)
ANY = pl.BlockSpec(memory_space=pl.ANY)
HBM = pl.BlockSpec(memory_space=pltpu.HBM)


def place(sides):
    e, g = lax.axis_index("expert"), lax.axis_index("group")
    z = g // sides
    return e, e & 1, (e >> 1) & 1, z, g % sides, (z ^ (z >> 1)) & 1


def visit(k, x, ab):
    return 2 * (ab if k % 2 == 0 else 1 - ab) + (x if k < 2 else 1 - x)


def call(kernel, out_shape, in_specs, args, scratch=(), limit=16, flops=0, size=0):
    many = isinstance(out_shape, list)
    return pl.pallas_call(
        kernel,
        out_shape=out_shape,
        in_specs=in_specs,
        out_specs=[VMEM] * len(out_shape) if many else VMEM,
        scratch_shapes=list(scratch),
        compiler_params=pltpu.CompilerParams(vmem_limit_bytes=limit << 20),
        cost_estimate=pl.CostEstimate(flops=flops, bytes_accessed=size, transcendentals=0),
    )(*args)


def pick_kernel(sides, visited, routing, mixing, tokens, *outs):
    picks, split = outs[:VISITS], outs[VISITS]
    _, _, x, _, _, ab = place(sides)
    rows = tokens.shape[0]
    lanes = lax.broadcasted_iota(jnp.int32, (rows, 128), 1)
    named, mix = routing[...], mixing[...]
    shares, members = [], jnp.zeros((rows, 128), F32)
    for k in range(VISITS):
        hit = named == visited[visit(k, x, ab)]
        shares.append(jnp.sum(jnp.where(hit, mix, 0.0), axis=1, keepdims=True))
        found = jnp.sum(jnp.where(hit, 1.0, 0.0), axis=1, keepdims=True)
        members = members + jnp.where(lanes == k, found, 0.0)
    above = lax.broadcasted_iota(jnp.int32, (rows, rows), 0) > lax.broadcasted_iota(
        jnp.int32, (rows, rows), 1
    )
    ranks = jnp.dot(
        jnp.where(above, 1.0, 0.0).astype(BF16), members.astype(BF16), preferred_element_type=F32
    )
    places = jnp.where(members > 0.5, ranks + (lanes * CAP).astype(F32), -1.0)
    slots = lax.broadcasted_iota(jnp.int32, (rows, VISITS * CAP), 1).astype(F32)
    spread = jnp.zeros((rows, VISITS * CAP), F32)
    for k in range(VISITS):
        spread = spread + jnp.where(slots == places[:, k : k + 1], shares[k], 0.0)
    top = spread.astype(BF16).astype(F32)
    split[...] = jnp.concatenate([top, spread - top], axis=1).astype(BF16)
    across = places.T
    slots = lax.broadcasted_iota(jnp.int32, (CAP, rows), 0).astype(F32)
    for k in range(VISITS):
        one = jnp.where(slots + float(CAP * k) == across[k : k + 1, :], 1.0, 0.0).astype(BF16)
        picks[k][...] = jnp.dot(one, tokens[...], preferred_element_type=F32).astype(BF16)


def merge_kernel(half, shares, *refs):
    pieces, out = refs[:VISITS], refs[-1]
    values = jnp.concatenate([piece[...] for piece in pieces] * 2, axis=0)
    out[...] = jnp.dot(shares[...], values, preferred_element_type=F32).astype(BF16)


def merge(half, shares, pieces, before):
    rows, (slots, width) = shares.shape[0], pieces[0].shape
    tile = width // 2
    ins = [pl.BlockSpec(shares.shape, lambda i, half: (0, 0))]
    ins += [pl.BlockSpec((slots, tile), lambda i, half: (0, i))] * VISITS
    args = [half, shares, *pieces]
    if before is not None:
        ins.append(ANY)
        args.append(before)
    return pl.pallas_call(
        merge_kernel,
        grid_spec=pltpu.PrefetchScalarGridSpec(
            num_scalar_prefetch=1,
            grid=(width // tile,),
            in_specs=ins,
            out_specs=pl.BlockSpec((rows, tile), lambda i, half: (0, half[0] * (width // tile) + i)),
        ),
        out_shape=jax.ShapeDtypeStruct((rows, 2 * width), BF16),
        input_output_aliases={} if before is None else {len(args) - 1: 0},
        compiler_params=pltpu.CompilerParams(vmem_limit_bytes=16 << 20),
    )(*args)


def cut_kernel(sides, held, axes, visited, *refs):
    count = len(axes)
    matrices, outs, sem = refs[:count], refs[count : 3 * count], refs[3 * count]
    _, c, x, _, _, ab = place(sides)
    copies = []
    for n, axis in enumerate(axes):
        mine, theirs = outs[2 * n], outs[2 * n + 1]
        size = mine.shape[axis + 1]
        for k in range(VISITS):
            local = lax.rem(visited[visit(k, x, ab)], held)
            for out, half in ((theirs, 1 - c), (mine, c)):
                part = pl.ds(pl.multiple_of(half * size, 128), size)
                source = matrices[n].at[local]
                source = source.at[part, :] if axis == 0 else source.at[:, part]
                copies.append(pltpu.make_async_copy(source, out.at[k], sem.at[len(copies)]))
    for copy in copies:
        copy.start()
    for copy in copies:
        copy.wait()


def cut(sides, visited, matrices, axes):
    shapes = []
    for matrix, axis in zip(matrices, axes):
        _, a, b = matrix.shape
        half = (VISITS, a // 2, b) if axis == 0 else (VISITS, a, b // 2)
        shapes += [jax.ShapeDtypeStruct(half, BF16)] * 2
    return call(
        functools.partial(cut_kernel, sides, matrices[0].shape[0], axes),
        shapes,
        [SMEM] + [HBM] * len(matrices),
        (visited, *(pltpu.with_memory_space_constraint(matrix, pltpu.HBM) for matrix in matrices)),
        [pltpu.SemaphoreType.DMA((2 * VISITS * len(matrices),))],
    )


def choose(own, out, here, there):
    @pl.when(own)
    def _():
        out[...] = here[...]

    @pl.when(jnp.logical_not(own))
    def _():
        out[...] = there[...]


def blend_kernel(sides, held, bit, visited, mine, theirs, got, mine_out, theirs_out):
    e, _, x, _, _, ab = place(sides)
    for k in range(VISITS):
        owner = visited[visit(k, x, ab)] // held
        own = (owner & bit) == (e & bit)
        choose(own, mine_out.at[k], mine.at[k], got.at[k])
        choose(own, theirs_out.at[k], theirs.at[k], got.at[VISITS + k])


def send_kernel(sides, held, ks, visited, mine, got, out):
    _, c, x, _, _, ab = place(sides)
    for n, k in enumerate(ks):
        owner = visited[visit(2 + k, x, ab)] // held
        choose((owner & 1) == c, out.at[n], mine.at[2 + k], got.at[2 + k])


def keep_kernel(sides, held, ks, visited, mine, got, far, *outs):
    _, c, x, _, _, ab = place(sides)
    for n, (k, out) in enumerate(zip(ks, outs)):
        owner = visited[visit(k, x, ab)] // held
        near = ((owner >> 1) & 1) == x

        @pl.when(near)
        def _():
            choose((owner & 1) == c, out, mine.at[k], got.at[k])

        @pl.when(jnp.logical_not(near))
        def _():
            out[...] = far[n]


def load_blocks(sides, keys, blocks, held, sem, down):
    _, c, _, z, y, _ = place(sides)
    copies = []
    for n, ((plane_bits, side_bits, core), block) in enumerate(zip(keys, blocks)):
        piece = (z ^ plane_bits) * sides + (y ^ side_bits)
        rows, columns = block.shape
        if down:
            piece = lax.rem(piece, 2 * sides)
            first = pl.ds(pl.multiple_of((c ^ core) * rows, 128), rows)
            spot = held.at[first, pl.ds(pl.multiple_of(piece * columns, 128), columns)]
        else:
            spot = held.at[pl.ds(pl.multiple_of(piece * rows, 128), rows), :]
        copies.append(pltpu.make_async_copy(block, spot, sem.at[n]))
    for copy in copies:
        copy.start()
    for copy in copies:
        copy.wait()


def gate_kernel(sides, keys, *refs):
    blocks, rows = refs[: len(keys)], refs[len(keys) : len(keys) + 2 * VISITS]
    out, held, sem = refs[len(keys) + 2 * VISITS :]
    load_blocks(sides, keys, blocks, held, sem, False)
    for side in range(2):
        picked = jnp.concatenate([ref[...] for ref in rows[side * VISITS : (side + 1) * VISITS]], axis=0)
        out[side] = jnp.dot(picked, held[...], preferred_element_type=F32)


def up_kernel(sides, keys, *refs):
    blocks, rows = refs[: len(keys)], refs[len(keys) : len(keys) + 2 * VISITS]
    gate, own, partner, held, sem = refs[len(keys) + 2 * VISITS :]
    load_blocks(sides, keys, blocks, held, sem, False)
    for side, out in enumerate((own, partner)):
        picked = jnp.concatenate([ref[...] for ref in rows[side * VISITS : (side + 1) * VISITS]], axis=0)
        up = jnp.dot(picked, held[...], preferred_element_type=F32)
        out[...] = (jax.nn.silu(gate[side]) * up).astype(BF16)


def down_kernel(sides, keys, *refs):
    count = len(keys)
    blocks, (own, partner), outs = refs[:count], refs[count : count + 2], refs[count + 2 : count + 2 + VISITS]
    held, hidden, sem = refs[count + 2 + VISITS :]
    _, c, _, _, _, _ = place(sides)
    inner = own.shape[1]
    hidden[:, pl.ds(pl.multiple_of(c * inner, 128), inner)] = own[...]
    hidden[:, pl.ds(pl.multiple_of((1 - c) * inner, 128), inner)] = partner[...]
    load_blocks(sides, keys, blocks, held, sem, True)
    out = jnp.dot(hidden[...], held[...], preferred_element_type=F32).astype(BF16)
    for k in range(VISITS):
        outs[k][...] = out[k * CAP : (k + 1) * CAP]


def body(mesh, tokens, routing, mixing, visited, gate_matrix, up_matrix, down_matrix):
    experts, groups = mesh.shape["expert"], mesh.shape["group"]
    planes = VISITS
    sides = groups // planes
    held = gate_matrix.shape[0]
    count, width = tokens.shape
    inner = gate_matrix.shape[2]
    total = VISITS * CAP
    shape = jax.ShapeDtypeStruct

    def swap(value, expert_bits=0, plane_bits=0, side_bits=0):
        pairs = []
        for one in range(experts):
            for two in range(groups):
                other = ((two // sides) ^ plane_bits) * sides + ((two % sides) ^ side_bits)
                pairs.append((one * groups + two, (one ^ expert_bits) * groups + other))
        return lax.ppermute(value, AXES, pairs)

    halves = list(cut(sides, visited, [gate_matrix], [1]))
    halves += cut(sides, visited, [up_matrix, down_matrix], [1, 0])
    matrices = []
    for n in range(3):
        mine, theirs = halves[2 * n : 2 * n + 2]
        bit = 4
        while bit < experts:
            got = swap(jnp.concatenate([mine, theirs], axis=0), expert_bits=bit)
            mine, theirs = call(
                functools.partial(blend_kernel, sides, held, bit),
                [shape(mine.shape, BF16)] * 2,
                [SMEM] + [VMEM] * 3,
                (visited, mine, theirs, got),
                limit=32,
            )
            bit *= 2
        matrices.append((mine, swap(theirs, expert_bits=1)))

    *picked, shares = call(
        functools.partial(pick_kernel, sides),
        [shape((CAP, width), BF16)] * VISITS + [shape((count, 2 * total), BF16)],
        [SMEM, VMEM, VMEM, VMEM],
        (visited, routing, mixing, tokens),
        limit=24,
    )

    sent = []
    for n, (mine, got) in enumerate(matrices):
        sent.append({})
        for ks in STEPS[n]:
            away = call(
                functools.partial(send_kernel, sides, held, ks),
                shape((len(ks), *mine.shape[1:]), BF16),
                [SMEM, VMEM, VMEM],
                (visited, mine, got),
            )
            sent[n][ks] = swap(away, expert_bits=2)
    rows = [
        picked[0],
        swap(picked[1], plane_bits=1),
        swap(picked[2], expert_bits=2),
        swap(picked[3], expert_bits=2, plane_bits=1),
    ]

    pieces = []
    for n, (mine, got) in enumerate(matrices):
        kept = {}
        for ks, far in sent[n].items():
            outs = call(
                functools.partial(keep_kernel, sides, held, ks),
                [shape(mine.shape[1:], BF16)] * len(ks),
                [SMEM] + [VMEM] * 3,
                (visited, mine, got, far),
            )
            kept.update(zip(ks, outs))
        same, other = kept[0], kept[1]
        found = [
            (0, same), (1, swap(other, plane_bits=1)), (2, swap(other, plane_bits=2)), (3, swap(same, plane_bits=3))
        ]
        keys, blocks = [], []
        for plane_bits, value in found:
            for side_bits in range(sides):
                moved = value
                if side_bits:
                    moved = swap(value, side_bits=side_bits)
                keys.append((plane_bits, side_bits, 0))
                blocks.append(moved)
                if n == 2:
                    keys.append((plane_bits, side_bits, 1))
                    blocks.append(swap(moved, expert_bits=1))
        pieces.append((keys, blocks))

    rows += [swap(value, expert_bits=1) for value in rows]
    keys, blocks = pieces[0]
    work = 4 * total * width * inner // 2
    gate = call(
        functools.partial(gate_kernel, sides, keys),
        shape((2, total, inner // 2), F32),
        [ANY] * len(keys) + [VMEM] * len(rows),
        (*blocks, *rows),
        [pltpu.VMEM((width, inner // 2), BF16), pltpu.SemaphoreType.DMA((len(keys),))],
        flops=work,
    )
    keys, blocks = pieces[1]
    own, partner = call(
        functools.partial(up_kernel, sides, keys),
        [shape((total, inner // 2), BF16)] * 2,
        [ANY] * len(keys) + [VMEM] * (len(rows) + 1),
        (*blocks, *rows, gate),
        [pltpu.VMEM((width, inner // 2), BF16), pltpu.SemaphoreType.DMA((len(keys),))],
        flops=work,
    )
    partner = swap(partner, expert_bits=1)
    keys, blocks = pieces[2]
    combined = None
    for part in range(2):
        chosen = [n for n, key in enumerate(keys) if key[0] // 2 == part]
        outs = call(
            functools.partial(down_kernel, sides, [keys[n] for n in chosen]),
            [shape((CAP, width // 2), BF16)] * VISITS,
            [ANY] * len(chosen) + [VMEM] * 2,
            (*(blocks[n] for n in chosen), own, partner),
            [
                pltpu.VMEM((inner, width // 2), BF16),
                pltpu.VMEM((total, inner), BF16),
                pltpu.SemaphoreType.DMA((len(chosen),)),
            ],
            flops=work // 2,
        )
        back = [
            outs[0],
            swap(outs[1], plane_bits=1),
            swap(outs[2], expert_bits=2),
            swap(outs[3], expert_bits=2, plane_bits=1),
        ]
        half = (lax.axis_index("group") // sides // 2) ^ part
        combined = merge(half.reshape(1), shares, back, combined)
    return combined


def solution(mesh):
    placed = (
        P(("expert", "group"), None),
        P(("expert", "group"), None),
        P(("expert", "group"), None),
        P(),
        P("expert", "group", None),
        P("expert", "group", None),
        P("expert", None, "group"),
    )
    return jax.shard_map(
        functools.partial(body, mesh),
        mesh=mesh,
        in_specs=placed,
        out_specs=P(("expert", "group"), None),
        check_vma=False,
    )
```

```python
import functools

import jax
import jax.numpy as jnp
from jax import lax
from jax.experimental import pallas as pl
from jax.experimental.pallas import tpu as pltpu
from jax.sharding import PartitionSpec as P


VISITS = 4
CAP = 80
AXES = ("expert", "group")
F32 = jnp.float32
BF16 = jnp.bfloat16


STEPS = (((1,), (0,)), ((1, 0),), ((1, 0),))

GROUPS = ((0, 1), (2, 3))

VMEM = pl.BlockSpec(memory_space=pltpu.VMEM)
SMEM = pl.BlockSpec(memory_space=pltpu.SMEM)
ANY = pl.BlockSpec(memory_space=pl.ANY)
HBM = pl.BlockSpec(memory_space=pltpu.HBM)


def place(sides):
    e, g = lax.axis_index("expert"), lax.axis_index("group")
    z = g // sides
    return e, e & 1, (e >> 1) & 1, z, g % sides, (z ^ (z >> 1)) & 1


def visit(k, x, ab):
    return 2 * (ab if k % 2 == 0 else 1 - ab) + (x if k < 2 else 1 - x)


def call(kernel, out_shape, in_specs, args, scratch=(), limit=8, flops=0):
    many = isinstance(out_shape, list)
    size = sum(array.size * array.dtype.itemsize for array in (*args, *(out_shape if many else [out_shape])))
    return pl.pallas_call(
        kernel,
        out_shape=out_shape,
        in_specs=in_specs,
        out_specs=[VMEM] * len(out_shape) if many else VMEM,
        scratch_shapes=list(scratch),
        compiler_params=pltpu.CompilerParams(vmem_limit_bytes=limit << 20),
        cost_estimate=pl.CostEstimate(flops=flops, bytes_accessed=size, transcendentals=0),
    )(*args)


def pick_kernel(sides, axes, visited, routing, mixing, tokens, *refs):
    count = len(axes)
    matrices, refs = refs[:count], refs[count:]
    picks, shares, refs = refs[:VISITS], refs[VISITS], refs[VISITS + 1 :]
    outs, (held, sem, cut_sem) = refs[: 2 * count], refs[2 * count :]
    copy = pltpu.make_async_copy(tokens, held, sem)
    copy.start()
    copies = []
    for n, (matrix, axis) in enumerate(zip(matrices, axes)):
        pair = outs[2 * n : 2 * n + 2]
        copies += cut_copies(sides, matrix.shape[0], axis, (0, 1), visited, matrix, pair, cut_sem.at[n])
    _, _, x, _, _, ab = place(sides)
    names, rows = routing.shape
    named, mix = routing[...], mixing[...]
    lines = lax.broadcasted_iota(jnp.int32, (names, rows), 0)
    weights, members = [], jnp.zeros((names, rows), F32)
    for k in range(VISITS):
        hit = named == visited[visit(k, x, ab)]
        weights.append(jnp.sum(jnp.where(hit, mix, 0.0), axis=0, keepdims=True))
        found = jnp.sum(jnp.where(hit, 1.0, 0.0), axis=0, keepdims=True)
        members = members + jnp.where(lines == k, found, 0.0)
    before = lax.broadcasted_iota(jnp.int32, (rows, rows), 0) < lax.broadcasted_iota(
        jnp.int32, (rows, rows), 1
    )
    ranks = jnp.dot(
        members.astype(BF16), jnp.where(before, 1.0, 0.0).astype(BF16), preferred_element_type=F32
    )
    places = jnp.where(members > 0.5, ranks, -1.0)
    slots = lax.broadcasted_iota(jnp.int32, (CAP, rows), 0).astype(F32)
    taken = [slots == places[k : k + 1, :] for k in range(VISITS)]
    copy.wait()
    for k in range(VISITS):
        one = jnp.where(taken[k], 1.0, 0.0).astype(BF16)
        picks[k][...] = jnp.dot(one, held[...], preferred_element_type=F32).astype(BF16)
    spread = jnp.concatenate([jnp.where(taken[k], weights[k], 0.0) for k in range(VISITS)], axis=0)
    top = spread.astype(BF16).astype(F32)
    shares[...] = jnp.concatenate([top, spread - top], axis=0).T.astype(BF16)
    for copy in copies:
        copy.wait()


def merge_kernel(half, parity, shares, *refs):
    pieces, out = refs[:-1], refs[-1]
    if len(pieces) >= 2 * VISITS:
        first = pl.program_id(0) == parity[0]
        values = []
        for k in range(VISITS):
            one, two = pieces[k][...], pieces[VISITS + k][...]
            values.append(jnp.where(first if k % 2 == 0 else jnp.logical_not(first), one, two))
    else:
        values = [piece[...] for piece in pieces[:VISITS]]
    out[...] = jnp.dot(shares[...], jnp.concatenate(values * 2, axis=0), preferred_element_type=F32).astype(BF16)


def merge(half, parity, shares, pieces, before, width):
    rows, tile = shares.shape[0], width // VISITS
    ins = [pl.BlockSpec(shares.shape, lambda i, half, parity: (0, 0))]
    for array, first, step in pieces:
        ins.append(
            pl.BlockSpec((array.shape[0], tile), lambda i, half, parity, first=first, step=step: (0, first + step * i))
        )
    args = [half, parity, shares, *(array for array, _, _ in pieces)]
    if before is not None:
        ins.append(ANY)
        args.append(before)
    return pl.pallas_call(
        merge_kernel,
        grid_spec=pltpu.PrefetchScalarGridSpec(
            num_scalar_prefetch=2,
            grid=(2,),
            in_specs=ins,
            out_specs=pl.BlockSpec((rows, tile), lambda i, half, parity: (0, half[0] * 2 + i)),
        ),
        out_shape=jax.ShapeDtypeStruct((rows, width), BF16),
        input_output_aliases={} if before is None else {len(args) - 1: 0},
        compiler_params=pltpu.CompilerParams(vmem_limit_bytes=8 << 20),
        cost_estimate=pl.CostEstimate(
            flops=4 * shares.size * tile, bytes_accessed=2 * shares.size * 2, transcendentals=0
        ),
    )(*args)


def cut_copies(sides, held, axis, halves, visited, matrix, outs, sem):
    _, c, x, _, _, ab = place(sides)
    size = outs[0].shape[axis + 1]
    copies = []
    for out, half in zip(outs, halves):
        part = pl.ds(pl.multiple_of((1 - c if half else c) * size, 128), size)
        for k in range(VISITS):
            source = matrix.at[lax.rem(visited[visit(k, x, ab)], held)]
            source = source.at[part, :] if axis == 0 else source.at[:, part]
            copies.append(pltpu.make_async_copy(source, out.at[k], sem.at[len(copies)]))
    for copy in copies:
        copy.start()
    return copies


def half_shape(matrix, axis):
    _, a, b = matrix.shape
    return jax.ShapeDtypeStruct((VISITS, a // 2, b) if axis == 0 else (VISITS, a, b // 2), BF16)


def cut_kernel(sides, held, axis, halves, visited, matrix, *refs):
    for copy in cut_copies(sides, held, axis, halves, visited, matrix, refs[:-1], refs[-1]):
        copy.wait()


def cut(sides, visited, matrix, axis, halves):
    return call(
        functools.partial(cut_kernel, sides, matrix.shape[0], axis, halves),
        [half_shape(matrix, axis)] * len(halves),
        [SMEM, HBM],
        (visited, pltpu.with_memory_space_constraint(matrix, pltpu.HBM)),
        [pltpu.SemaphoreType.DMA((VISITS * len(halves),))],
        limit=2,
    )


def choose(own, out, here, there):
    @pl.when(own)
    def _():
        out[...] = here[...]

    @pl.when(jnp.logical_not(own))
    def _():
        out[...] = there[...]


def blend_kernel(sides, held, bit, visited, mine, theirs, got, mine_out, theirs_out):
    e, _, x, _, _, ab = place(sides)
    for k in range(VISITS):
        owner = visited[visit(k, x, ab)] // held
        own = (owner & bit) == (e & bit)
        choose(own, mine_out.at[k], mine.at[k], got.at[k])
        choose(own, theirs_out.at[k], theirs.at[k], got.at[VISITS + k])


def send_kernel(sides, held, ks, visited, mine, got, out):
    _, c, x, _, _, ab = place(sides)
    for n, k in enumerate(ks):
        owner = visited[visit(2 + k, x, ab)] // held
        choose((owner & 1) == c, out.at[n], mine.at[2 + k], got.at[2 + k])


def keep_kernel(sides, held, ks, visited, mine, got, far, *outs):
    _, c, x, _, _, ab = place(sides)
    for n, (k, out) in enumerate(zip(ks, outs)):
        owner = visited[visit(k, x, ab)] // held
        near = ((owner >> 1) & 1) == x

        @pl.when(near)
        def _():
            choose((owner & 1) == c, out, mine.at[k], got.at[k])

        @pl.when(jnp.logical_not(near))
        def _():
            out[...] = far[n]


def load_blocks(sides, keys, blocks, held, sem, spots=None):
    _, c, _, z, y, _ = place(sides)
    copies = []
    for n, ((plane_bits, side_bits, core), block) in enumerate(zip(keys, blocks)):
        rows, columns = block.shape
        if spots is None:
            piece = (z ^ plane_bits) * sides + (y ^ side_bits)
            spot = held.at[pl.ds(pl.multiple_of(piece * rows, 128), rows), :]
        else:
            tile, moves = spots[plane_bits]
            piece = (tile + ((z ^ plane_bits) & 1 if moves else 0)) * sides + (y ^ side_bits)
            first = pl.ds(pl.multiple_of((c ^ core) * rows, 128), rows)
            spot = held.at[first, pl.ds(pl.multiple_of(piece * columns, 128), columns)]
        copies.append(pltpu.make_async_copy(block, spot, sem.at[n]))
    for copy in copies:
        copy.start()
    for copy in copies:
        copy.wait()


def gate_kernel(sides, keys, *refs):
    blocks, rows = refs[: len(keys)], refs[len(keys) : len(keys) + 2 * VISITS]
    out, held, sem = refs[len(keys) + 2 * VISITS :]
    load_blocks(sides, keys, blocks, held, sem)
    for side in range(2):
        picked = jnp.concatenate([ref[...] for ref in rows[side * VISITS : (side + 1) * VISITS]], axis=0)
        out[side] = jnp.dot(picked, held[...], preferred_element_type=F32)


def up_kernel(sides, keys, *refs):
    blocks, rows = refs[: len(keys)], refs[len(keys) : len(keys) + 2 * VISITS]
    gate, own, partner, held, sem = refs[len(keys) + 2 * VISITS :]
    load_blocks(sides, keys, blocks, held, sem)
    for side, out in enumerate((own, partner)):
        picked = jnp.concatenate([ref[...] for ref in rows[side * VISITS : (side + 1) * VISITS]], axis=0)
        up = jnp.dot(picked, held[...], preferred_element_type=F32)
        out[...] = (jax.nn.silu(gate[side]) * up).astype(BF16)


def down_kernel(sides, keys, spots, *refs):
    count = len(keys)
    blocks, (own, partner), outs = refs[:count], refs[count : count + 2], refs[count + 2 : count + 2 + VISITS]
    held, hidden, sem = refs[count + 2 + VISITS :]
    _, c, _, _, _, _ = place(sides)
    inner = own.shape[1]
    hidden[:, pl.ds(pl.multiple_of(c * inner, 128), inner)] = own[...]
    hidden[:, pl.ds(pl.multiple_of((1 - c) * inner, 128), inner)] = partner[...]
    load_blocks(sides, keys, blocks, held, sem, spots)
    out = jnp.dot(hidden[...], held[...], preferred_element_type=F32).astype(BF16)
    for k in range(VISITS):
        outs[k][...] = out[k * CAP : (k + 1) * CAP]


def body(mesh, tokens, routing, mixing, visited, gate_matrix, up_matrix, down_matrix):
    experts, groups = mesh.shape["expert"], mesh.shape["group"]
    planes = VISITS
    sides = groups // planes
    held = gate_matrix.shape[0]
    count, width = tokens.shape
    inner = gate_matrix.shape[2]
    total = VISITS * CAP
    shape = jax.ShapeDtypeStruct
    z = lax.axis_index("group") // sides

    def swap(value, expert_bits=0, plane_bits=0, side_bits=0):
        pairs = []
        for one in range(experts):
            for two in range(groups):
                other = ((two // sides) ^ plane_bits) * sides + ((two % sides) ^ side_bits)
                pairs.append((one * groups + two, (one ^ expert_bits) * groups + other))
        return lax.ppermute(value, AXES, pairs)

    (theirs,) = cut(sides, visited, gate_matrix, 1, (1,))
    (mine,) = cut(sides, visited, gate_matrix, 1, (0,))
    others, axes = (up_matrix, down_matrix), (1, 0)
    outs = call(
        functools.partial(pick_kernel, sides, axes),
        [shape((CAP, width), BF16)] * VISITS
        + [shape((count, 2 * total), BF16)]
        + [half_shape(matrix, axis) for matrix, axis in zip(others, axes) for _ in range(2)],
        [SMEM, VMEM, VMEM] + [HBM] * 3,
        (
            visited,
            routing.T,
            mixing.T,
            *(pltpu.with_memory_space_constraint(array, pltpu.HBM) for array in (tokens, *others)),
        ),
        [
            pltpu.VMEM(tokens.shape, BF16),
            pltpu.SemaphoreType.DMA,
            pltpu.SemaphoreType.DMA((2, 2 * VISITS)),
        ],
        limit=12,
    )
    picked, shares = outs[:VISITS], outs[VISITS]
    matrices = []
    for mine, theirs in ((mine, theirs), outs[VISITS + 1 : VISITS + 3], outs[VISITS + 3 :]):
        bit = 4
        while bit < experts:
            got = swap(jnp.concatenate([mine, theirs], axis=0), expert_bits=bit)
            mine, theirs = call(
                functools.partial(blend_kernel, sides, held, bit),
                [shape(mine.shape, BF16)] * 2,
                [SMEM] + [VMEM] * 3,
                (visited, mine, theirs, got),
                limit=32,
            )
            bit *= 2
        matrices.append((mine, swap(theirs, expert_bits=1)))

    sent = []
    for n, (mine, got) in enumerate(matrices):
        sent.append({})
        for ks in STEPS[n]:
            away = call(
                functools.partial(send_kernel, sides, held, ks),
                shape((len(ks), *mine.shape[1:]), BF16),
                [SMEM, VMEM, VMEM],
                (visited, mine, got),
                limit=2,
            )
            sent[n][ks] = swap(away, expert_bits=2)
    rows = [
        picked[0],
        swap(picked[1], plane_bits=1),
        swap(picked[2], expert_bits=2),
        swap(picked[3], expert_bits=2, plane_bits=1),
    ]

    pieces = []
    for n, (mine, got) in enumerate(matrices):
        kept = {}
        for ks, far in sent[n].items():
            outs = call(
                functools.partial(keep_kernel, sides, held, ks),
                [shape(mine.shape[1:], BF16)] * len(ks),
                [SMEM] + [VMEM] * 3,
                (visited, mine, got, far),
                limit=2,
            )
            kept.update(zip(ks, outs))
        same, other = kept[0], kept[1]
        found = [
            (0, same), (1, swap(other, plane_bits=1)), (2, swap(other, plane_bits=2)), (3, swap(same, plane_bits=3))
        ]
        keys, blocks = [], []
        for plane_bits, value in found:
            for side_bits in range(sides):
                moved = value
                if side_bits:
                    moved = swap(value, side_bits=side_bits)
                keys.append((plane_bits, side_bits, 0))
                blocks.append(moved)
                if n == 2:
                    keys.append((plane_bits, side_bits, 1))
                    blocks.append(swap(moved, expert_bits=1))
        pieces.append((keys, blocks))

    rows += [swap(value, expert_bits=1) for value in rows]
    keys, blocks = pieces[0]
    work = 4 * total * width * inner // 2
    gate = call(
        functools.partial(gate_kernel, sides, keys),
        shape((2, total, inner // 2), F32),
        [ANY] * len(keys) + [VMEM] * len(rows),
        (*blocks, *rows),
        [pltpu.VMEM((width, inner // 2), BF16), pltpu.SemaphoreType.DMA((len(keys),))],
        flops=work,
    )
    keys, blocks = pieces[1]
    own, partner = call(
        functools.partial(up_kernel, sides, keys),
        [shape((total, inner // 2), BF16)] * 2,
        [ANY] * len(keys) + [VMEM] * (len(rows) + 1),
        (*blocks, *rows, gate),
        [pltpu.VMEM((width, inner // 2), BF16), pltpu.SemaphoreType.DMA((len(keys),))],
        flops=work,
    )
    partner = swap(partner, expert_bits=1)
    keys, blocks = pieces[2]
    parity, near, far = ((value).reshape(1) for value in (z % 2, z // 2, 1 - z // 2))
    found = {}
    for group in GROUPS:
        spots = {}
        for plane in group:
            moves = plane ^ 1 in group
            spots[plane] = (spots[plane ^ 1][0] if plane ^ 1 in spots else len(spots), moves)
        chosen = [n for n, key in enumerate(keys) if key[0] in group]
        columns = len(group) * width // planes
        outs = call(
            functools.partial(down_kernel, sides, [keys[n] for n in chosen], spots),
            [shape((CAP, columns), BF16)] * VISITS,
            [ANY] * len(chosen) + [VMEM] * 2,
            (*(blocks[n] for n in chosen), own, partner),
            [
                pltpu.VMEM((inner, columns), BF16),
                pltpu.VMEM((total, inner), BF16),
                pltpu.SemaphoreType.DMA((len(chosen),)),
            ],
            flops=work * len(group) // planes,
        )
        back = [
            outs[0],
            swap(outs[1], plane_bits=1),
            swap(outs[2], expert_bits=2),
            swap(outs[3], expert_bits=2, plane_bits=1),
        ]
        for plane in group:
            found[plane] = [(array, spots[plane][0], int(spots[plane][1])) for array in back]
    combined = merge(near, parity, shares, found[0], None, width)
    last = found[2] if found[2][0][2] else found[2] + found[3]
    combined = merge(far, parity, shares, last, combined, width)
    return combined


def solution(mesh):
    placed = (
        P(("expert", "group"), None),
        P(("expert", "group"), None),
        P(("expert", "group"), None),
        P(),
        P("expert", "group", None),
        P("expert", "group", None),
        P("expert", None, "group"),
    )
    return jax.shard_map(
        functools.partial(body, mesh),
        mesh=mesh,
        in_specs=placed,
        out_specs=P(("expert", "group"), None),
        check_vma=False,
    )
```

```python
import functools

import jax
import jax.numpy as jnp
from jax import lax
from jax.experimental import pallas as pl
from jax.experimental.pallas import tpu as pltpu
from jax.sharding import PartitionSpec as P


VISITS = 4
CAP = 80
AXES = ("expert", "group")
F32 = jnp.float32
BF16 = jnp.bfloat16


STEPS = (((1,), (0,)), ((1, 0),), ((1, 0),))

GROUPS = ((0, 1), (2, 3))

VMEM = pl.BlockSpec(memory_space=pltpu.VMEM)
SMEM = pl.BlockSpec(memory_space=pltpu.SMEM)
ANY = pl.BlockSpec(memory_space=pl.ANY)
HBM = pl.BlockSpec(memory_space=pltpu.HBM)


def place(sides):
    e, g = lax.axis_index("expert"), lax.axis_index("group")
    z = g // sides
    return e, e & 1, (e >> 1) & 1, z, g % sides, (z ^ (z >> 1)) & 1


def visit(k, x, ab):
    return 2 * (ab if k % 2 == 0 else 1 - ab) + (x if k < 2 else 1 - x)


def call(kernel, out_shape, in_specs, args, scratch=(), limit=8, flops=0):
    many = isinstance(out_shape, list)
    size = sum(array.size * array.dtype.itemsize for array in (*args, *(out_shape if many else [out_shape])))
    return pl.pallas_call(
        kernel,
        out_shape=out_shape,
        in_specs=in_specs,
        out_specs=[VMEM] * len(out_shape) if many else VMEM,
        scratch_shapes=list(scratch),
        compiler_params=pltpu.CompilerParams(vmem_limit_bytes=limit << 20),
        cost_estimate=pl.CostEstimate(flops=flops, bytes_accessed=size, transcendentals=0),
    )(*args)


def pick_kernel(sides, axes, visited, routing, mixing, tokens, *refs):
    count = len(axes)
    matrices, refs = refs[:count], refs[count:]
    picks, shares, refs = refs[:VISITS], refs[VISITS], refs[VISITS + 1 :]
    outs, (held, sem, cut_sem) = refs[: 2 * count], refs[2 * count :]
    copy = pltpu.make_async_copy(tokens, held, sem)
    copy.start()
    copies = []
    for n, (matrix, axis) in enumerate(zip(matrices, axes)):
        pair = outs[2 * n : 2 * n + 2]
        copies += cut_copies(sides, matrix.shape[0], axis, (0, 1), visited, matrix, pair, cut_sem.at[n])
    _, _, x, _, _, ab = place(sides)
    names, rows = routing.shape
    named, mix = routing[...], mixing[...]
    lines = lax.broadcasted_iota(jnp.int32, (names, rows), 0)
    weights, members = [], jnp.zeros((names, rows), F32)
    for k in range(VISITS):
        hit = named == visited[visit(k, x, ab)]
        weights.append(jnp.sum(jnp.where(hit, mix, 0.0), axis=0, keepdims=True))
        found = jnp.sum(jnp.where(hit, 1.0, 0.0), axis=0, keepdims=True)
        members = members + jnp.where(lines == k, found, 0.0)
    before = lax.broadcasted_iota(jnp.int32, (rows, rows), 0) < lax.broadcasted_iota(
        jnp.int32, (rows, rows), 1
    )
    ranks = jnp.dot(
        members.astype(BF16), jnp.where(before, 1.0, 0.0).astype(BF16), preferred_element_type=F32
    )
    places = jnp.where(members > 0.5, ranks, -1.0)
    slots = lax.broadcasted_iota(jnp.int32, (CAP, rows), 0).astype(F32)
    taken = [slots == places[k : k + 1, :] for k in range(VISITS)]
    copy.wait()
    ones = jnp.concatenate([jnp.where(mask, 1.0, 0.0) for mask in taken], axis=0).astype(BF16)
    found = jnp.dot(ones, held[...], preferred_element_type=F32).astype(BF16)
    for k in range(VISITS):
        picks[k][...] = found[k * CAP : (k + 1) * CAP]
    spread = jnp.concatenate([jnp.where(taken[k], weights[k], 0.0) for k in range(VISITS)], axis=0)
    top = spread.astype(BF16).astype(F32)
    shares[...] = jnp.concatenate([top, spread - top], axis=0).T.astype(BF16)
    for copy in copies:
        copy.wait()


def merge_kernel(half, parity, shares, *refs):
    pieces, out = refs[:-1], refs[-1]
    if len(pieces) >= 2 * VISITS:
        first = pl.program_id(0) == parity[0]
        values = []
        for k in range(VISITS):
            one, two = pieces[k][...], pieces[VISITS + k][...]
            values.append(jnp.where(first if k % 2 == 0 else jnp.logical_not(first), one, two))
    else:
        values = [piece[...] for piece in pieces[:VISITS]]
    out[...] = jnp.dot(shares[...], jnp.concatenate(values * 2, axis=0), preferred_element_type=F32).astype(BF16)


def merge(half, parity, shares, pieces, before, width):
    rows, tile = shares.shape[0], width // VISITS
    ins = [pl.BlockSpec(shares.shape, lambda i, half, parity: (0, 0))]
    for array, first, step in pieces:
        ins.append(
            pl.BlockSpec((array.shape[0], tile), lambda i, half, parity, first=first, step=step: (0, first + step * i))
        )
    args = [half, parity, shares, *(array for array, _, _ in pieces)]
    if before is not None:
        ins.append(ANY)
        args.append(before)
    return pl.pallas_call(
        merge_kernel,
        grid_spec=pltpu.PrefetchScalarGridSpec(
            num_scalar_prefetch=2,
            grid=(2,),
            in_specs=ins,
            out_specs=pl.BlockSpec((rows, tile), lambda i, half, parity: (0, half[0] * 2 + i)),
        ),
        out_shape=jax.ShapeDtypeStruct((rows, width), BF16),
        input_output_aliases={} if before is None else {len(args) - 1: 0},
        compiler_params=pltpu.CompilerParams(vmem_limit_bytes=8 << 20),
        cost_estimate=pl.CostEstimate(
            flops=4 * shares.size * tile, bytes_accessed=2 * shares.size * 2, transcendentals=0
        ),
    )(*args)


def cut_copies(sides, held, axis, halves, visited, matrix, outs, sem):
    _, c, x, _, _, ab = place(sides)
    size = outs[0].shape[axis + 1]
    copies = []
    for out, half in zip(outs, halves):
        part = pl.ds(pl.multiple_of((1 - c if half else c) * size, 128), size)
        for k in range(VISITS):
            source = matrix.at[lax.rem(visited[visit(k, x, ab)], held)]
            source = source.at[part, :] if axis == 0 else source.at[:, part]
            copies.append(pltpu.make_async_copy(source, out.at[k], sem.at[len(copies)]))
    for copy in copies:
        copy.start()
    return copies


def half_shape(matrix, axis):
    _, a, b = matrix.shape
    return jax.ShapeDtypeStruct((VISITS, a // 2, b) if axis == 0 else (VISITS, a, b // 2), BF16)


def cut_kernel(sides, held, axis, halves, visited, matrix, *refs):
    for copy in cut_copies(sides, held, axis, halves, visited, matrix, refs[:-1], refs[-1]):
        copy.wait()


def cut(sides, visited, matrix, axis, halves):
    return call(
        functools.partial(cut_kernel, sides, matrix.shape[0], axis, halves),
        [half_shape(matrix, axis)] * len(halves),
        [SMEM, HBM],
        (visited, pltpu.with_memory_space_constraint(matrix, pltpu.HBM)),
        [pltpu.SemaphoreType.DMA((VISITS * len(halves),))],
        limit=2,
    )


def choose(own, out, here, there):
    @pl.when(own)
    def _():
        out[...] = here[...]

    @pl.when(jnp.logical_not(own))
    def _():
        out[...] = there[...]


def blend_kernel(sides, held, bit, visited, mine, theirs, got, mine_out, theirs_out):
    e, _, x, _, _, ab = place(sides)
    for k in range(VISITS):
        owner = visited[visit(k, x, ab)] // held
        own = (owner & bit) == (e & bit)
        choose(own, mine_out.at[k], mine.at[k], got.at[k])
        choose(own, theirs_out.at[k], theirs.at[k], got.at[VISITS + k])


def send_kernel(sides, held, ks, visited, mine, got, out):
    _, c, x, _, _, ab = place(sides)
    for n, k in enumerate(ks):
        owner = visited[visit(2 + k, x, ab)] // held
        choose((owner & 1) == c, out.at[n], mine.at[2 + k], got.at[2 + k])


def keep_kernel(sides, held, ks, visited, mine, got, far, *outs):
    _, c, x, _, _, ab = place(sides)
    for n, (k, out) in enumerate(zip(ks, outs)):
        owner = visited[visit(k, x, ab)] // held
        near = ((owner >> 1) & 1) == x

        @pl.when(near)
        def _():
            choose((owner & 1) == c, out, mine.at[k], got.at[k])

        @pl.when(jnp.logical_not(near))
        def _():
            out[...] = far[n]


def product(sides, keys, blocks, rows):
    _, _, _, z, y, _ = place(sides)
    total = None
    for (plane_bits, side_bits, _), block in zip(keys, blocks):
        size = block.shape[0]
        piece = pl.ds(pl.multiple_of(((z ^ plane_bits) * sides + (y ^ side_bits)) * size, 128), size)
        part = jnp.dot(
            jnp.concatenate([ref[:, piece] for ref in rows], axis=0), block[...], preferred_element_type=F32
        )
        total = part if total is None else total + part
    return total


def gate_kernel(sides, keys, *refs):
    blocks, rows, out = refs[: len(keys)], refs[len(keys) : len(keys) + 2 * VISITS], refs[-1]
    for side in range(2):
        out[side] = product(sides, keys, blocks, rows[side * VISITS : (side + 1) * VISITS])


def up_kernel(sides, keys, *refs):
    blocks, rows = refs[: len(keys)], refs[len(keys) : len(keys) + 2 * VISITS]
    gate, own, partner = refs[len(keys) + 2 * VISITS :]
    for side, out in enumerate((own, partner)):
        up = product(sides, keys, blocks, rows[side * VISITS : (side + 1) * VISITS])
        out[...] = (jax.nn.silu(gate[side]) * up).astype(BF16)


def down_kernel(sides, keys, spots, *refs):
    count = len(keys)
    blocks, hidden, outs = refs[:count], refs[count : count + 2], refs[count + 2 :]
    _, _, _, z, y, _ = place(sides)
    pairs = {}
    for (plane_bits, side_bits, core), block in zip(keys, blocks):
        pairs.setdefault((plane_bits, side_bits), {})[core] = block
    for (plane_bits, side_bits), pair in pairs.items():
        part = jnp.dot(hidden[0][...], pair[0][...], preferred_element_type=F32)
        part = (part + jnp.dot(hidden[1][...], pair[1][...], preferred_element_type=F32)).astype(BF16)
        columns = part.shape[1]
        tile, moves = spots[plane_bits]
        piece = (tile + ((z ^ plane_bits) & 1 if moves else 0)) * sides + (y ^ side_bits)
        for k in range(VISITS):
            outs[k][:, pl.ds(pl.multiple_of(piece * columns, 128), columns)] = part[k * CAP : (k + 1) * CAP]


def body(mesh, tokens, routing, mixing, visited, gate_matrix, up_matrix, down_matrix):
    experts, groups = mesh.shape["expert"], mesh.shape["group"]
    planes = VISITS
    sides = groups // planes
    held = gate_matrix.shape[0]
    count, width = tokens.shape
    inner = gate_matrix.shape[2]
    total = VISITS * CAP
    shape = jax.ShapeDtypeStruct
    z = lax.axis_index("group") // sides

    def swap(value, expert_bits=0, plane_bits=0, side_bits=0):
        pairs = []
        for one in range(experts):
            for two in range(groups):
                other = ((two // sides) ^ plane_bits) * sides + ((two % sides) ^ side_bits)
                pairs.append((one * groups + two, (one ^ expert_bits) * groups + other))
        return lax.ppermute(value, AXES, pairs)

    theirs, mine = cut(sides, visited, gate_matrix, 1, (1, 0))
    others, axes = (up_matrix, down_matrix), (1, 0)
    outs = call(
        functools.partial(pick_kernel, sides, axes),
        [shape((CAP, width), BF16)] * VISITS
        + [shape((count, 2 * total), BF16)]
        + [half_shape(matrix, axis) for matrix, axis in zip(others, axes) for _ in range(2)],
        [SMEM, VMEM, VMEM] + [HBM] * 3,
        (
            visited,
            routing.T,
            mixing.T,
            *(pltpu.with_memory_space_constraint(array, pltpu.HBM) for array in (tokens, *others)),
        ),
        [
            pltpu.VMEM(tokens.shape, BF16),
            pltpu.SemaphoreType.DMA,
            pltpu.SemaphoreType.DMA((2, 2 * VISITS)),
        ],
        limit=12,
    )
    picked, shares = outs[:VISITS], outs[VISITS]
    matrices = []
    for mine, theirs in ((mine, theirs), outs[VISITS + 1 : VISITS + 3], outs[VISITS + 3 :]):
        bit = 4
        while bit < experts:
            got = swap(jnp.concatenate([mine, theirs], axis=0), expert_bits=bit)
            mine, theirs = call(
                functools.partial(blend_kernel, sides, held, bit),
                [shape(mine.shape, BF16)] * 2,
                [SMEM] + [VMEM] * 3,
                (visited, mine, theirs, got),
                limit=32,
            )
            bit *= 2
        matrices.append((mine, swap(theirs, expert_bits=1)))

    sent = []
    for n, (mine, got) in enumerate(matrices):
        sent.append({})
        for ks in STEPS[n]:
            away = call(
                functools.partial(send_kernel, sides, held, ks),
                shape((len(ks), *mine.shape[1:]), BF16),
                [SMEM, VMEM, VMEM],
                (visited, mine, got),
                limit=2,
            )
            sent[n][ks] = swap(away, expert_bits=2)
    rows = [
        picked[0],
        swap(picked[1], plane_bits=1),
        swap(picked[2], expert_bits=2),
        swap(picked[3], expert_bits=2, plane_bits=1),
    ]

    pieces = []
    for n, (mine, got) in enumerate(matrices):
        kept = {}
        for ks, far in sent[n].items():
            outs = call(
                functools.partial(keep_kernel, sides, held, ks),
                [shape(mine.shape[1:], BF16)] * len(ks),
                [SMEM] + [VMEM] * 3,
                (visited, mine, got, far),
                limit=2,
            )
            kept.update(zip(ks, outs))
        same, other = kept[0], kept[1]
        found = [
            (0, same), (1, swap(other, plane_bits=1)), (2, swap(other, plane_bits=2)), (3, swap(same, plane_bits=3))
        ]
        keys, blocks = [], []
        for plane_bits, value in found:
            for side_bits in range(sides):
                moved = value
                if side_bits:
                    moved = swap(value, side_bits=side_bits)
                keys.append((plane_bits, side_bits, 0))
                blocks.append(moved)
                if n == 2:
                    keys.append((plane_bits, side_bits, 1))
                    blocks.append(swap(moved, expert_bits=1))
        pieces.append((keys, blocks))

    rows += [swap(value, expert_bits=1) for value in rows]
    keys, blocks = pieces[0]
    work = 4 * total * width * inner // 2
    gate = call(
        functools.partial(gate_kernel, sides, keys),
        shape((2, total, inner // 2), F32),
        [VMEM] * (len(keys) + len(rows)),
        (*blocks, *rows),
        flops=work,
    )
    keys, blocks = pieces[1]
    own, partner = call(
        functools.partial(up_kernel, sides, keys),
        [shape((total, inner // 2), BF16)] * 2,
        [VMEM] * (len(keys) + len(rows) + 1),
        (*blocks, *rows, gate),
        flops=work,
    )
    partner = swap(partner, expert_bits=1)
    keys, blocks = pieces[2]
    parity, near, far = ((value).reshape(1) for value in (z % 2, z // 2, 1 - z // 2))
    found = {}
    for group in GROUPS:
        spots = {}
        for plane in group:
            moves = plane ^ 1 in group
            spots[plane] = (spots[plane ^ 1][0] if plane ^ 1 in spots else len(spots), moves)
        chosen = [n for n, key in enumerate(keys) if key[0] in group]
        columns = len(group) * width // planes
        outs = call(
            functools.partial(down_kernel, sides, [keys[n] for n in chosen], spots),
            [shape((CAP, columns), BF16)] * VISITS,
            [VMEM] * (len(chosen) + 2),
            (*(blocks[n] for n in chosen), own, partner),
            flops=work * len(group) // planes,
        )
        back = [
            outs[0],
            swap(outs[1], plane_bits=1),
            swap(outs[2], expert_bits=2),
            swap(outs[3], expert_bits=2, plane_bits=1),
        ]
        for plane in group:
            found[plane] = [(array, spots[plane][0], int(spots[plane][1])) for array in back]
    combined = merge(near, parity, shares, found[0], None, width)
    last = found[2] if found[2][0][2] else found[2] + found[3]
    combined = merge(far, parity, shares, last, combined, width)
    return combined


def solution(mesh):
    placed = (
        P(("expert", "group"), None),
        P(("expert", "group"), None),
        P(("expert", "group"), None),
        P(),
        P("expert", "group", None),
        P("expert", "group", None),
        P("expert", None, "group"),
    )
    return jax.shard_map(
        functools.partial(body, mesh),
        mesh=mesh,
        in_specs=placed,
        out_specs=P(("expert", "group"), None),
        check_vma=False,
    )
```

```python
import functools

import jax
import jax.numpy as jnp
from jax import lax
from jax.experimental import pallas as pl
from jax.experimental.pallas import tpu as pltpu
from jax.sharding import PartitionSpec as P


VISITS = 4
CAP = 80
AXES = ("expert", "group")
F32 = jnp.float32
BF16 = jnp.bfloat16


STEPS = (((1,), (0,)), ((1, 0),), ((1, 0),))

GROUPS = ((0, 1), (2,), (3,))

VMEM = pl.BlockSpec(memory_space=pltpu.VMEM)
SMEM = pl.BlockSpec(memory_space=pltpu.SMEM)
ANY = pl.BlockSpec(memory_space=pl.ANY)
HBM = pl.BlockSpec(memory_space=pltpu.HBM)


def place(sides):
    e, g = lax.axis_index("expert"), lax.axis_index("group")
    z = g // sides
    return e, e & 1, (e >> 1) & 1, z, g % sides, (z ^ (z >> 1)) & 1


def visit(k, x, ab):
    return 2 * (ab if k % 2 == 0 else 1 - ab) + (x if k < 2 else 1 - x)


def call(kernel, out_shape, in_specs, args, scratch=(), limit=8, flops=0):
    many = isinstance(out_shape, list)
    size = sum(array.size * array.dtype.itemsize for array in (*args, *(out_shape if many else [out_shape])))
    return pl.pallas_call(
        kernel,
        out_shape=out_shape,
        in_specs=in_specs,
        out_specs=[VMEM] * len(out_shape) if many else VMEM,
        scratch_shapes=list(scratch),
        compiler_params=pltpu.CompilerParams(vmem_limit_bytes=limit << 20),
        cost_estimate=pl.CostEstimate(flops=flops, bytes_accessed=size, transcendentals=0),
    )(*args)


def pick_kernel(sides, axes, visited, routing, mixing, tokens, *refs):
    count = len(axes)
    matrices, refs = refs[:count], refs[count:]
    picks, shares, refs = refs[:VISITS], refs[VISITS], refs[VISITS + 1 :]
    outs, (held, sem, cut_sem) = refs[: 2 * count], refs[2 * count :]
    copy = pltpu.make_async_copy(tokens, held, sem)
    copy.start()
    copies = []
    for n, (matrix, axis) in enumerate(zip(matrices, axes)):
        pair = outs[2 * n : 2 * n + 2]
        copies += cut_copies(sides, matrix.shape[0], axis, (0, 1), visited, matrix, pair, cut_sem.at[n])
    _, _, x, _, _, ab = place(sides)
    names, rows = routing.shape
    named, mix = routing[...], mixing[...]
    lines = lax.broadcasted_iota(jnp.int32, (names, rows), 0)
    weights, members = [], jnp.zeros((names, rows), F32)
    for k in range(VISITS):
        hit = named == visited[visit(k, x, ab)]
        weights.append(jnp.sum(jnp.where(hit, mix, 0.0), axis=0, keepdims=True))
        found = jnp.sum(jnp.where(hit, 1.0, 0.0), axis=0, keepdims=True)
        members = members + jnp.where(lines == k, found, 0.0)
    before = lax.broadcasted_iota(jnp.int32, (rows, rows), 0) < lax.broadcasted_iota(
        jnp.int32, (rows, rows), 1
    )
    ranks = jnp.dot(
        members.astype(BF16), jnp.where(before, 1.0, 0.0).astype(BF16), preferred_element_type=F32
    )
    places = jnp.where(members > 0.5, ranks, -1.0)
    slots = lax.broadcasted_iota(jnp.int32, (CAP, rows), 0).astype(F32)
    taken = [slots == places[k : k + 1, :] for k in range(VISITS)]
    copy.wait()
    ones = jnp.concatenate([jnp.where(mask, 1.0, 0.0) for mask in taken], axis=0).astype(BF16)
    found = jnp.dot(ones, held[...], preferred_element_type=F32).astype(BF16)
    for k in range(VISITS):
        picks[k][...] = found[k * CAP : (k + 1) * CAP]
    spread = jnp.concatenate([jnp.where(taken[k], weights[k], 0.0) for k in range(VISITS)], axis=0)
    top = spread.astype(BF16).astype(F32)
    shares[...] = jnp.concatenate([top, spread - top], axis=0).T.astype(BF16)
    for copy in copies:
        copy.wait()


def merge_kernel(half, parity, shares, *refs):
    pieces, out = refs[:-1], refs[-1]
    if len(pieces) >= 2 * VISITS:
        first = pl.program_id(0) == parity[0]
        values = []
        for k in range(VISITS):
            one, two = pieces[k][...], pieces[VISITS + k][...]
            values.append(jnp.where(first if k % 2 == 0 else jnp.logical_not(first), one, two))
    else:
        values = [piece[...] for piece in pieces[:VISITS]]
    out[...] = jnp.dot(shares[...], jnp.concatenate(values * 2, axis=0), preferred_element_type=F32).astype(BF16)


def merge(half, parity, shares, pieces, before, width):
    rows, tile = shares.shape[0], width // VISITS
    ins = [pl.BlockSpec(shares.shape, lambda i, half, parity: (0, 0))]
    for array, first, step in pieces:
        ins.append(
            pl.BlockSpec((array.shape[0], tile), lambda i, half, parity, first=first, step=step: (0, first + step * i))
        )
    args = [half, parity, shares, *(array for array, _, _ in pieces)]
    if before is not None:
        ins.append(ANY)
        args.append(before)
    return pl.pallas_call(
        merge_kernel,
        grid_spec=pltpu.PrefetchScalarGridSpec(
            num_scalar_prefetch=2,
            grid=(2,),
            in_specs=ins,
            out_specs=pl.BlockSpec((rows, tile), lambda i, half, parity: (0, half[0] * 2 + i)),
        ),
        out_shape=jax.ShapeDtypeStruct((rows, width), BF16),
        input_output_aliases={} if before is None else {len(args) - 1: 0},
        compiler_params=pltpu.CompilerParams(vmem_limit_bytes=8 << 20),
        cost_estimate=pl.CostEstimate(
            flops=4 * shares.size * tile, bytes_accessed=2 * shares.size * 2, transcendentals=0
        ),
    )(*args)


def cut_copies(sides, held, axis, halves, visited, matrix, outs, sem):
    _, c, x, _, _, ab = place(sides)
    size = outs[0].shape[axis + 1]
    copies = []
    for out, half in zip(outs, halves):
        part = pl.ds(pl.multiple_of((1 - c if half else c) * size, 128), size)
        for k in range(VISITS):
            source = matrix.at[lax.rem(visited[visit(k, x, ab)], held)]
            source = source.at[part, :] if axis == 0 else source.at[:, part]
            copies.append(pltpu.make_async_copy(source, out.at[k], sem.at[len(copies)]))
    for copy in copies:
        copy.start()
    return copies


def half_shape(matrix, axis):
    _, a, b = matrix.shape
    return jax.ShapeDtypeStruct((VISITS, a // 2, b) if axis == 0 else (VISITS, a, b // 2), BF16)


def cut_kernel(sides, held, axis, halves, visited, matrix, *refs):
    for copy in cut_copies(sides, held, axis, halves, visited, matrix, refs[:-1], refs[-1]):
        copy.wait()


def cut(sides, visited, matrix, axis, halves):
    return call(
        functools.partial(cut_kernel, sides, matrix.shape[0], axis, halves),
        [half_shape(matrix, axis)] * len(halves),
        [SMEM, HBM],
        (visited, pltpu.with_memory_space_constraint(matrix, pltpu.HBM)),
        [pltpu.SemaphoreType.DMA((VISITS * len(halves),))],
        limit=2,
    )


def choose(own, out, here, there):
    @pl.when(own)
    def _():
        out[...] = here[...]

    @pl.when(jnp.logical_not(own))
    def _():
        out[...] = there[...]


def blend_kernel(sides, held, bit, visited, mine, theirs, got, mine_out, theirs_out):
    e, _, x, _, _, ab = place(sides)
    for k in range(VISITS):
        owner = visited[visit(k, x, ab)] // held
        own = (owner & bit) == (e & bit)
        choose(own, mine_out.at[k], mine.at[k], got.at[k])
        choose(own, theirs_out.at[k], theirs.at[k], got.at[VISITS + k])


def send_kernel(sides, held, ks, visited, mine, got, out):
    _, c, x, _, _, ab = place(sides)
    for n, k in enumerate(ks):
        owner = visited[visit(2 + k, x, ab)] // held
        choose((owner & 1) == c, out.at[n], mine.at[2 + k], got.at[2 + k])


def keep_kernel(sides, held, ks, visited, mine, got, far, *outs):
    _, c, x, _, _, ab = place(sides)
    for n, (k, out) in enumerate(zip(ks, outs)):
        owner = visited[visit(k, x, ab)] // held
        near = ((owner >> 1) & 1) == x

        @pl.when(near)
        def _():
            choose((owner & 1) == c, out, mine.at[k], got.at[k])

        @pl.when(jnp.logical_not(near))
        def _():
            out[...] = far[n]


def product(sides, keys, blocks, rows):
    _, _, _, z, y, _ = place(sides)
    total = None
    for (plane_bits, side_bits, _), block in zip(keys, blocks):
        size = block.shape[0]
        piece = pl.ds(pl.multiple_of(((z ^ plane_bits) * sides + (y ^ side_bits)) * size, 128), size)
        part = jnp.dot(
            jnp.concatenate([ref[:, piece] for ref in rows], axis=0), block[...], preferred_element_type=F32
        )
        total = part if total is None else total + part
    return total


def gate_kernel(sides, keys, *refs):
    blocks, rows, out = refs[: len(keys)], refs[len(keys) : len(keys) + 2 * VISITS], refs[-1]
    for side in range(2):
        out[side] = product(sides, keys, blocks, rows[side * VISITS : (side + 1) * VISITS])


def up_kernel(sides, keys, *refs):
    blocks, rows = refs[: len(keys)], refs[len(keys) : len(keys) + 2 * VISITS]
    gate, own, partner = refs[len(keys) + 2 * VISITS :]
    for side, out in enumerate((own, partner)):
        up = product(sides, keys, blocks, rows[side * VISITS : (side + 1) * VISITS])
        out[...] = (jax.nn.silu(gate[side]) * up).astype(BF16)


def down_kernel(sides, keys, spots, *refs):
    count = len(keys)
    blocks, hidden, outs = refs[:count], refs[count : count + 2], refs[count + 2 :]
    _, _, _, z, y, _ = place(sides)
    pairs = {}
    for (plane_bits, side_bits, core), block in zip(keys, blocks):
        pairs.setdefault((plane_bits, side_bits), {})[core] = block
    for (plane_bits, side_bits), pair in pairs.items():
        part = jnp.dot(hidden[0][...], pair[0][...], preferred_element_type=F32)
        part = (part + jnp.dot(hidden[1][...], pair[1][...], preferred_element_type=F32)).astype(BF16)
        columns = part.shape[1]
        tile, moves = spots[plane_bits]
        piece = (tile + ((z ^ plane_bits) & 1 if moves else 0)) * sides + (y ^ side_bits)
        for k in range(VISITS):
            outs[k][:, pl.ds(pl.multiple_of(piece * columns, 128), columns)] = part[k * CAP : (k + 1) * CAP]


def body(mesh, tokens, routing, mixing, visited, gate_matrix, up_matrix, down_matrix):
    experts, groups = mesh.shape["expert"], mesh.shape["group"]
    planes = VISITS
    sides = groups // planes
    held = gate_matrix.shape[0]
    count, width = tokens.shape
    inner = gate_matrix.shape[2]
    total = VISITS * CAP
    shape = jax.ShapeDtypeStruct
    z = lax.axis_index("group") // sides

    def swap(value, expert_bits=0, plane_bits=0, side_bits=0):
        pairs = []
        for one in range(experts):
            for two in range(groups):
                other = ((two // sides) ^ plane_bits) * sides + ((two % sides) ^ side_bits)
                pairs.append((one * groups + two, (one ^ expert_bits) * groups + other))
        return lax.ppermute(value, AXES, pairs)

    theirs, mine = cut(sides, visited, gate_matrix, 1, (1, 0))
    others, axes = (up_matrix,), (1,)
    outs = call(
        functools.partial(pick_kernel, sides, axes),
        [shape((CAP, width), BF16)] * VISITS
        + [shape((count, 2 * total), BF16)]
        + [half_shape(matrix, axis) for matrix, axis in zip(others, axes) for _ in range(2)],
        [SMEM, VMEM, VMEM] + [HBM] * (1 + len(others)),
        (
            visited,
            routing.T,
            mixing.T,
            *(pltpu.with_memory_space_constraint(array, pltpu.HBM) for array in (tokens, *others)),
        ),
        [
            pltpu.VMEM(tokens.shape, BF16),
            pltpu.SemaphoreType.DMA,
            pltpu.SemaphoreType.DMA((len(others), 2 * VISITS)),
        ],
        limit=12,
    )
    picked, shares = outs[:VISITS], outs[VISITS]
    downs = cut(sides, visited, down_matrix, 0, (0, 1))
    matrices = []
    for mine, theirs in ((mine, theirs), outs[VISITS + 1 :], downs):
        bit = 4
        while bit < experts:
            got = swap(jnp.concatenate([mine, theirs], axis=0), expert_bits=bit)
            mine, theirs = call(
                functools.partial(blend_kernel, sides, held, bit),
                [shape(mine.shape, BF16)] * 2,
                [SMEM] + [VMEM] * 3,
                (visited, mine, theirs, got),
                limit=32,
            )
            bit *= 2
        matrices.append((mine, swap(theirs, expert_bits=1)))

    sent = []
    for n, (mine, got) in enumerate(matrices):
        sent.append({})
        for ks in STEPS[n]:
            away = call(
                functools.partial(send_kernel, sides, held, ks),
                shape((len(ks), *mine.shape[1:]), BF16),
                [SMEM, VMEM, VMEM],
                (visited, mine, got),
                limit=2,
            )
            sent[n][ks] = swap(away, expert_bits=2)
    rows = [
        picked[0],
        swap(picked[1], plane_bits=1),
        swap(picked[2], expert_bits=2),
        swap(picked[3], expert_bits=2, plane_bits=1),
    ]

    pieces = []
    for n, (mine, got) in enumerate(matrices):
        kept = {}
        for ks, far in sent[n].items():
            outs = call(
                functools.partial(keep_kernel, sides, held, ks),
                [shape(mine.shape[1:], BF16)] * len(ks),
                [SMEM] + [VMEM] * 3,
                (visited, mine, got, far),
                limit=2,
            )
            kept.update(zip(ks, outs))
        same, other = kept[0], kept[1]
        found = [
            (0, same), (1, swap(other, plane_bits=1)), (2, swap(other, plane_bits=2)), (3, swap(same, plane_bits=3))
        ]
        keys, blocks = [], []
        for plane_bits, value in found:
            for side_bits in range(sides):
                moved = value
                if side_bits:
                    moved = swap(value, side_bits=side_bits)
                keys.append((plane_bits, side_bits, 0))
                blocks.append(moved)
                if n == 2:
                    keys.append((plane_bits, side_bits, 1))
                    blocks.append(swap(moved, expert_bits=1))
        pieces.append((keys, blocks))

    rows += [swap(value, expert_bits=1) for value in rows]
    keys, blocks = pieces[0]
    work = 4 * total * width * inner // 2
    gate = call(
        functools.partial(gate_kernel, sides, keys),
        shape((2, total, inner // 2), F32),
        [VMEM] * (len(keys) + len(rows)),
        (*blocks, *rows),
        flops=work,
    )
    keys, blocks = pieces[1]
    own, partner = call(
        functools.partial(up_kernel, sides, keys),
        [shape((total, inner // 2), BF16)] * 2,
        [VMEM] * (len(keys) + len(rows) + 1),
        (*blocks, *rows, gate),
        flops=work,
    )
    partner = swap(partner, expert_bits=1)
    keys, blocks = pieces[2]
    parity, near, far = ((value).reshape(1) for value in (z % 2, z // 2, 1 - z // 2))
    found = {}
    for group in GROUPS:
        spots = {}
        for plane in group:
            moves = plane ^ 1 in group
            spots[plane] = (spots[plane ^ 1][0] if plane ^ 1 in spots else len(spots), moves)
        chosen = [n for n, key in enumerate(keys) if key[0] in group]
        columns = len(group) * width // planes
        outs = call(
            functools.partial(down_kernel, sides, [keys[n] for n in chosen], spots),
            [shape((CAP, columns), BF16)] * VISITS,
            [VMEM] * (len(chosen) + 2),
            (*(blocks[n] for n in chosen), own, partner),
            flops=work * len(group) // planes,
        )
        back = [
            outs[0],
            swap(outs[1], plane_bits=1),
            swap(outs[2], expert_bits=2),
            swap(outs[3], expert_bits=2, plane_bits=1),
        ]
        for plane in group:
            found[plane] = [(array, spots[plane][0], int(spots[plane][1])) for array in back]
    combined = merge(near, parity, shares, found[0], None, width)
    last = found[2] if found[2][0][2] else found[2] + found[3]
    combined = merge(far, parity, shares, last, combined, width)
    return combined


def solution(mesh):
    placed = (
        P(("expert", "group"), None),
        P(("expert", "group"), None),
        P(("expert", "group"), None),
        P(),
        P("expert", "group", None),
        P("expert", "group", None),
        P("expert", None, "group"),
    )
    return jax.shard_map(
        functools.partial(body, mesh),
        mesh=mesh,
        in_specs=placed,
        out_specs=P(("expert", "group"), None),
        check_vma=False,
    )
```

```python
import functools

import jax
import jax.numpy as jnp
from jax import lax
from jax.experimental import pallas as pl
from jax.experimental.pallas import tpu as pltpu
from jax.sharding import PartitionSpec as P


VISITS = 4
CAP = 80
CUTS = 2
AXES = ("expert", "group")
F32 = jnp.float32
BF16 = jnp.bfloat16


STEPS = (((1,), (0,)), ((1, 0),), ((1, 0),))

GROUPS = ((0, 1), (2,), (3,))

VMEM = pl.BlockSpec(memory_space=pltpu.VMEM)
SMEM = pl.BlockSpec(memory_space=pltpu.SMEM)
ANY = pl.BlockSpec(memory_space=pl.ANY)
HBM = pl.BlockSpec(memory_space=pltpu.HBM)


def place(sides):
    e, g = lax.axis_index("expert"), lax.axis_index("group")
    z = g // sides
    return e, e & 1, (e >> 1) & 1, z, g % sides, (z ^ (z >> 1)) & 1


def visit(k, x, ab):
    return 2 * (ab if k % 2 == 0 else 1 - ab) + (x if k < 2 else 1 - x)


def call(kernel, out_shape, in_specs, args, scratch=(), limit=8, flops=0):
    many = isinstance(out_shape, list)
    size = sum(array.size * array.dtype.itemsize for array in (*args, *(out_shape if many else [out_shape])))
    return pl.pallas_call(
        kernel,
        out_shape=out_shape,
        in_specs=in_specs,
        out_specs=[VMEM] * len(out_shape) if many else VMEM,
        scratch_shapes=list(scratch),
        compiler_params=pltpu.CompilerParams(vmem_limit_bytes=limit << 20),
        cost_estimate=pl.CostEstimate(flops=flops, bytes_accessed=size, transcendentals=0),
    )(*args)


def pick_kernel(sides, axes, visited, routing, mixing, tokens, *refs):
    count = len(axes)
    matrices, refs = refs[:count], refs[count:]
    picks, shares, refs = refs[:VISITS], refs[VISITS], refs[VISITS + 1 :]
    outs, (held, sem, cut_sem) = refs[: 2 * count], refs[2 * count :]
    copy = pltpu.make_async_copy(tokens, held, sem)
    copy.start()
    copies = []
    for n, (matrix, axis) in enumerate(zip(matrices, axes)):
        pair = outs[2 * n : 2 * n + 2]
        copies += cut_copies(sides, matrix.shape[0], axis, (0, 1), visited, matrix, pair, cut_sem.at[n])
    _, _, x, _, _, ab = place(sides)
    names, rows = routing.shape
    named, mix = routing[...], mixing[...]
    lines = lax.broadcasted_iota(jnp.int32, (names, rows), 0)
    weights, members = [], jnp.zeros((names, rows), F32)
    for k in range(VISITS):
        hit = named == visited[visit(k, x, ab)]
        weights.append(jnp.sum(jnp.where(hit, mix, 0.0), axis=0, keepdims=True))
        found = jnp.sum(jnp.where(hit, 1.0, 0.0), axis=0, keepdims=True)
        members = members + jnp.where(lines == k, found, 0.0)
    before = lax.broadcasted_iota(jnp.int32, (rows, rows), 0) < lax.broadcasted_iota(
        jnp.int32, (rows, rows), 1
    )
    ranks = jnp.dot(
        members.astype(BF16), jnp.where(before, 1.0, 0.0).astype(BF16), preferred_element_type=F32
    )
    places = jnp.where(members > 0.5, ranks, -1.0)
    slots = lax.broadcasted_iota(jnp.int32, (CAP, rows), 0).astype(F32)
    taken = [slots == places[k : k + 1, :] for k in range(VISITS)]
    copy.wait()
    ones = jnp.concatenate([jnp.where(mask, 1.0, 0.0) for mask in taken], axis=0).astype(BF16)
    found = jnp.dot(ones, held[...], preferred_element_type=F32).astype(BF16)
    for k in range(VISITS):
        picks[k][...] = found[k * CAP : (k + 1) * CAP]
    spread = jnp.concatenate([jnp.where(taken[k], weights[k], 0.0) for k in range(VISITS)], axis=0)
    top = spread.astype(BF16).astype(F32)
    shares[...] = jnp.concatenate([top, spread - top], axis=0).T.astype(BF16)
    for copy in copies:
        copy.wait()


def merge_kernel(half, parity, shares, *refs):
    pieces, out = refs[:-1], refs[-1]
    if len(pieces) >= 2 * VISITS:
        first = pl.program_id(0) // CUTS == parity[0]
        values = []
        for k in range(VISITS):
            one, two = pieces[k][...], pieces[VISITS + k][...]
            values.append(jnp.where(first if k % 2 == 0 else jnp.logical_not(first), one, two))
    else:
        values = [piece[...] for piece in pieces[:VISITS]]
    out[...] = jnp.dot(shares[...], jnp.concatenate(values * 2, axis=0), preferred_element_type=F32).astype(BF16)


def merge(half, parity, shares, pieces, before, width):
    rows, tile = shares.shape[0], width // VISITS // CUTS
    ins = [pl.BlockSpec(shares.shape, lambda i, half, parity: (0, 0))]
    for array, first, step in pieces:
        ins.append(
            pl.BlockSpec((array.shape[0], tile), lambda i, half, parity, first=first, step=step: (0, (first + step * (i // CUTS)) * CUTS + i % CUTS))
        )
    args = [half, parity, shares, *(array for array, _, _ in pieces)]
    if before is not None:
        ins.append(ANY)
        args.append(before)
    return pl.pallas_call(
        merge_kernel,
        grid_spec=pltpu.PrefetchScalarGridSpec(
            num_scalar_prefetch=2,
            grid=(2 * CUTS,),
            in_specs=ins,
            out_specs=pl.BlockSpec((rows, tile), lambda i, half, parity: (0, half[0] * 2 * CUTS + i)),
        ),
        out_shape=jax.ShapeDtypeStruct((rows, width), BF16),
        input_output_aliases={} if before is None else {len(args) - 1: 0},
        compiler_params=pltpu.CompilerParams(vmem_limit_bytes=8 << 20),
        cost_estimate=pl.CostEstimate(
            flops=4 * shares.size * tile, bytes_accessed=2 * shares.size * 2, transcendentals=0
        ),
    )(*args)


def cut_copies(sides, held, axis, halves, visited, matrix, outs, sem):
    _, c, x, _, _, ab = place(sides)
    size = outs[0].shape[axis + 1]
    copies = []
    for out, half in zip(outs, halves):
        part = pl.ds(pl.multiple_of((1 - c if half else c) * size, 128), size)
        for k in range(VISITS):
            source = matrix.at[lax.rem(visited[visit(k, x, ab)], held)]
            source = source.at[part, :] if axis == 0 else source.at[:, part]
            copies.append(pltpu.make_async_copy(source, out.at[k], sem.at[len(copies)]))
    for copy in copies:
        copy.start()
    return copies


def half_shape(matrix, axis):
    _, a, b = matrix.shape
    return jax.ShapeDtypeStruct((VISITS, a // 2, b) if axis == 0 else (VISITS, a, b // 2), BF16)


def cut_kernel(sides, held, axis, halves, visited, matrix, *refs):
    for copy in cut_copies(sides, held, axis, halves, visited, matrix, refs[:-1], refs[-1]):
        copy.wait()


def cut(sides, visited, matrix, axis, halves):
    return call(
        functools.partial(cut_kernel, sides, matrix.shape[0], axis, halves),
        [half_shape(matrix, axis)] * len(halves),
        [SMEM, HBM],
        (visited, pltpu.with_memory_space_constraint(matrix, pltpu.HBM)),
        [pltpu.SemaphoreType.DMA((VISITS * len(halves),))],
        limit=2,
    )


def choose(own, out, here, there):
    @pl.when(own)
    def _():
        out[...] = here[...]

    @pl.when(jnp.logical_not(own))
    def _():
        out[...] = there[...]


def blend_kernel(sides, held, bit, visited, mine, theirs, got, mine_out, theirs_out):
    e, _, x, _, _, ab = place(sides)
    for k in range(VISITS):
        owner = visited[visit(k, x, ab)] // held
        own = (owner & bit) == (e & bit)
        choose(own, mine_out.at[k], mine.at[k], got.at[k])
        choose(own, theirs_out.at[k], theirs.at[k], got.at[VISITS + k])


def send_kernel(sides, held, ks, visited, mine, got, out):
    _, c, x, _, _, ab = place(sides)
    for n, k in enumerate(ks):
        owner = visited[visit(2 + k, x, ab)] // held
        choose((owner & 1) == c, out.at[n], mine.at[2 + k], got.at[2 + k])


def keep_kernel(sides, held, ks, visited, mine, got, far, *outs):
    _, c, x, _, _, ab = place(sides)
    for n, (k, out) in enumerate(zip(ks, outs)):
        owner = visited[visit(k, x, ab)] // held
        near = ((owner >> 1) & 1) == x

        @pl.when(near)
        def _():
            choose((owner & 1) == c, out, mine.at[k], got.at[k])

        @pl.when(jnp.logical_not(near))
        def _():
            out[...] = far[n]


def product(sides, keys, blocks, rows):
    _, _, _, z, y, _ = place(sides)
    total = None
    for (plane_bits, side_bits, _), block in zip(keys, blocks):
        size = block.shape[0]
        piece = pl.ds(pl.multiple_of(((z ^ plane_bits) * sides + (y ^ side_bits)) * size, 128), size)
        part = jnp.dot(
            jnp.concatenate([ref[:, piece] for ref in rows], axis=0), block[...], preferred_element_type=F32
        )
        total = part if total is None else total + part
    return total


def gate_kernel(sides, keys, *refs):
    blocks, rows, out = refs[: len(keys)], refs[len(keys) : len(keys) + 2 * VISITS], refs[-1]
    for side in range(2):
        out[side] = product(sides, keys, blocks, rows[side * VISITS : (side + 1) * VISITS])


def up_kernel(sides, keys, *refs):
    blocks, rows = refs[: len(keys)], refs[len(keys) : len(keys) + 2 * VISITS]
    gate, own, partner = refs[len(keys) + 2 * VISITS :]
    for side, out in enumerate((own, partner)):
        up = product(sides, keys, blocks, rows[side * VISITS : (side + 1) * VISITS])
        out[...] = (jax.nn.silu(gate[side]) * up).astype(BF16)


def down_kernel(sides, keys, spots, *refs):
    count = len(keys)
    blocks, hidden, outs = refs[:count], refs[count : count + 2], refs[count + 2 :]
    _, _, _, z, y, _ = place(sides)
    pairs = {}
    for (plane_bits, side_bits, core), block in zip(keys, blocks):
        pairs.setdefault((plane_bits, side_bits), {})[core] = block
    for (plane_bits, side_bits), pair in pairs.items():
        part = jnp.dot(hidden[0][...], pair[0][...], preferred_element_type=F32)
        part = (part + jnp.dot(hidden[1][...], pair[1][...], preferred_element_type=F32)).astype(BF16)
        columns = part.shape[1]
        tile, moves = spots[plane_bits]
        piece = (tile + ((z ^ plane_bits) & 1 if moves else 0)) * sides + (y ^ side_bits)
        for k in range(VISITS):
            outs[k][:, pl.ds(pl.multiple_of(piece * columns, 128), columns)] = part[k * CAP : (k + 1) * CAP]


def body(mesh, tokens, routing, mixing, visited, gate_matrix, up_matrix, down_matrix):
    experts, groups = mesh.shape["expert"], mesh.shape["group"]
    planes = VISITS
    sides = groups // planes
    held = gate_matrix.shape[0]
    count, width = tokens.shape
    inner = gate_matrix.shape[2]
    total = VISITS * CAP
    shape = jax.ShapeDtypeStruct
    z = lax.axis_index("group") // sides

    def swap(value, expert_bits=0, plane_bits=0, side_bits=0):
        pairs = []
        for one in range(experts):
            for two in range(groups):
                other = ((two // sides) ^ plane_bits) * sides + ((two % sides) ^ side_bits)
                pairs.append((one * groups + two, (one ^ expert_bits) * groups + other))
        return lax.ppermute(value, AXES, pairs)

    theirs, mine = cut(sides, visited, gate_matrix, 1, (1, 0))
    others, axes = (up_matrix,), (1,)
    outs = call(
        functools.partial(pick_kernel, sides, axes),
        [shape((CAP, width), BF16)] * VISITS
        + [shape((count, 2 * total), BF16)]
        + [half_shape(matrix, axis) for matrix, axis in zip(others, axes) for _ in range(2)],
        [SMEM, VMEM, VMEM] + [HBM] * (1 + len(others)),
        (
            visited,
            routing.T,
            mixing.T,
            *(pltpu.with_memory_space_constraint(array, pltpu.HBM) for array in (tokens, *others)),
        ),
        [
            pltpu.VMEM(tokens.shape, BF16),
            pltpu.SemaphoreType.DMA,
            pltpu.SemaphoreType.DMA((len(others), 2 * VISITS)),
        ],
        limit=12,
    )
    picked, shares = outs[:VISITS], outs[VISITS]
    downs = cut(sides, visited, down_matrix, 0, (0, 1))
    matrices = []
    for mine, theirs in ((mine, theirs), outs[VISITS + 1 :], downs):
        bit = 4
        while bit < experts:
            got = swap(jnp.concatenate([mine, theirs], axis=0), expert_bits=bit)
            mine, theirs = call(
                functools.partial(blend_kernel, sides, held, bit),
                [shape(mine.shape, BF16)] * 2,
                [SMEM] + [VMEM] * 3,
                (visited, mine, theirs, got),
                limit=32,
            )
            bit *= 2
        matrices.append((mine, swap(theirs, expert_bits=1)))

    sent = []
    for n, (mine, got) in enumerate(matrices):
        sent.append({})
        for ks in STEPS[n]:
            away = call(
                functools.partial(send_kernel, sides, held, ks),
                shape((len(ks), *mine.shape[1:]), BF16),
                [SMEM, VMEM, VMEM],
                (visited, mine, got),
                limit=2,
            )
            sent[n][ks] = swap(away, expert_bits=2)
    rows = [
        picked[0],
        swap(picked[1], plane_bits=1),
        swap(picked[2], expert_bits=2),
        swap(picked[3], expert_bits=2, plane_bits=1),
    ]

    pieces = []
    for n, (mine, got) in enumerate(matrices):
        kept = {}
        for ks, far in sent[n].items():
            outs = call(
                functools.partial(keep_kernel, sides, held, ks),
                [shape(mine.shape[1:], BF16)] * len(ks),
                [SMEM] + [VMEM] * 3,
                (visited, mine, got, far),
                limit=2,
            )
            kept.update(zip(ks, outs))
        same, other = kept[0], kept[1]
        found = [
            (0, same), (1, swap(other, plane_bits=1)), (2, swap(other, plane_bits=2)), (3, swap(same, plane_bits=3))
        ]
        keys, blocks = [], []
        for plane_bits, value in found:
            for side_bits in range(sides):
                moved = value
                if side_bits:
                    moved = swap(value, side_bits=side_bits)
                keys.append((plane_bits, side_bits, 0))
                blocks.append(moved)
                if n == 2:
                    keys.append((plane_bits, side_bits, 1))
                    blocks.append(swap(moved, expert_bits=1))
        pieces.append((keys, blocks))

    rows += [swap(value, expert_bits=1) for value in rows]
    keys, blocks = pieces[0]
    work = 4 * total * width * inner // 2
    gate = call(
        functools.partial(gate_kernel, sides, keys),
        shape((2, total, inner // 2), F32),
        [VMEM] * (len(keys) + len(rows)),
        (*blocks, *rows),
        flops=work,
    )
    keys, blocks = pieces[1]
    own, partner = call(
        functools.partial(up_kernel, sides, keys),
        [shape((total, inner // 2), BF16)] * 2,
        [VMEM] * (len(keys) + len(rows) + 1),
        (*blocks, *rows, gate),
        flops=work,
    )
    partner = swap(partner, expert_bits=1)
    keys, blocks = pieces[2]
    parity, near, far = ((value).reshape(1) for value in (z % 2, z // 2, 1 - z // 2))
    found = {}
    for group in GROUPS:
        spots = {}
        for plane in group:
            moves = plane ^ 1 in group
            spots[plane] = (spots[plane ^ 1][0] if plane ^ 1 in spots else len(spots), moves)
        chosen = [n for n, key in enumerate(keys) if key[0] in group]
        columns = len(group) * width // planes
        outs = call(
            functools.partial(down_kernel, sides, [keys[n] for n in chosen], spots),
            [shape((CAP, columns), BF16)] * VISITS,
            [VMEM] * (len(chosen) + 2),
            (*(blocks[n] for n in chosen), own, partner),
            flops=work * len(group) // planes,
        )
        back = [
            outs[0],
            swap(outs[1], plane_bits=1),
            swap(outs[2], expert_bits=2),
            swap(outs[3], expert_bits=2, plane_bits=1),
        ]
        for plane in group:
            found[plane] = [(array, spots[plane][0], int(spots[plane][1])) for array in back]
    combined = merge(near, parity, shares, found[0], None, width)
    last = found[2] if found[2][0][2] else found[2] + found[3]
    combined = merge(far, parity, shares, last, combined, width)
    return combined


def solution(mesh):
    placed = (
        P(("expert", "group"), None),
        P(("expert", "group"), None),
        P(("expert", "group"), None),
        P(),
        P("expert", "group", None),
        P("expert", "group", None),
        P("expert", None, "group"),
    )
    return jax.shard_map(
        functools.partial(body, mesh),
        mesh=mesh,
        in_specs=placed,
        out_specs=P(("expert", "group"), None),
        check_vma=False,
    )
```
